32 devices in a mesh: view: 4 (over x, core), bx: 4 (over z), by: 2 (over y).
Axes of the slice: x: 2, y: 2, z: 4, core: 2. Of those that a mesh axis runs over, the one named last changes fastest.
Arguments:
- estimate: float32 [256, 32, 128], P('bx', 'by'), may hold values from 0.5 to 2
- observed: float32 [4, 2048, 512], P('view', ('bx', 'by')), may hold values from 0.25 to 4
- destination: int32 [4, 2048, 1], P('view', ('bx', 'by')), may hold values from 0 to 7; in each aligned block of 256 rows (0 to 255, 256 to 511, ..., all dimensions but the last counted through in order) at most 64 rows name the same one
- slot_index: int32 [4, 2048], P('view', ('bx', 'by')), may hold values from 0 to 255
- valid_count: int32 [4, 2048], P('view', ('bx', 'by')), may hold values from 32 to 128
- blend_weight: float32 [4, 2048], P('view', ('bx', 'by')), may hold values from 0.2 to 1
- kernel_x: float32 [4, 17], P('view'), may hold values from 0.1 to 1
- kernel_y: float32 [4, 17], P('view'), may hold values from 0.1 to 1
- kernel_z: float32 [4, 33], P('view'), may hold values from 0.1 to 1
Outputs:
- updated: float32 [256, 32, 128], P('bx', 'by')
The draws below stay inside these ranges and needn't reach their ends.
Inputs may be any that keep to these rules, and one draw needn't show every extreme that they name: `destination`: in each view, the 256 rows of one device name no brick more than 64 times, a bound that some block reaches.
All inputs are finite; a program needn't handle non-finite values.
Results may differ from the reference program's by a relative error of at most 0.0001.
Values sent between devices are 32-bit elements; how exact they have to be, the bound alone decides.
No kernel may reach another device: no remote copies, remote signals or barrier semaphores. Data moves between devices by JAX's collectives and lax.ppermute only.
A program may use at most 64 MiB of HBM per device.

```python
import math
import jax
import jax.numpy as jnp
import numpy as np
from jax import lax

CX = 64
CY = 16
CZ = 128
R = 8
RZ = 16
YP = 4
VIEWS = 4
NB = 8
NX = 256
NY = 32
NZ = 128
PV = 512
SLOTS = 256
PIECES = 256
CAP = 64
N_BX = 4
N_BY = 2


def place_ends(array, own_key, low, largest):
    dims = array.shape
    index_at = [jax.random.randint(jax.random.fold_in(own_key, axis), (), 0, dims[axis]) for axis in range(len(dims))]
    array = array.at[tuple(index_at)].set(low)
    longest = dims.index(max(dims))
    index_at[longest] = (index_at[longest] + 1) % dims[longest]
    return array.at[tuple(index_at)].set(largest)


def block_scale(stream_key, shape, pieces, least, high):
    loudness, own = 1.0, jax.random.fold_in(stream_key, 6)
    for dim, blocks in pieces:
        draws = jnp.exp(jax.random.uniform(jax.random.fold_in(own, dim), (blocks,), jnp.float32, least / len(pieces), high / len(pieces)))
        loudness = loudness * jnp.repeat(draws, shape[dim] // blocks).reshape([-1 if axis == dim else 1 for axis in range(len(shape))])
    return loudness


def shared_out(key, own, number, rows, number_of, top, most, lean):
    order = jax.random.permutation(key, number_of)
    packed, common = portions_of(number_of, rows * top, most, lean, True), portions_of(number_of, rows * top, most, lean, False)
    places = jnp.arange(number_of)

    def named(lengths, offset_by):
        used = int((lengths > 0).sum())
        fixed = max(1, used // 4)
        passed = fixed + (places - fixed + offset_by * (used - fixed)) % max(1, number_of - fixed)
        return jnp.zeros((number_of,), jnp.int32).at[order[jnp.where(places < fixed, places, passed)]].set(jnp.asarray(lengths, jnp.int32))

    lengths = jnp.where(number % 4 == 0, named(packed, number // 4), named(common, number - number // 4 - 1))
    mixed = jax.random.permutation(jax.random.fold_in(own, 3), number_of)
    source_of, taker = mixed[0:number_of // 2 * 2:2], mixed[1:number_of // 2 * 2:2]
    margin = jnp.minimum(lengths[source_of] - 1, most - lengths[taker]) // 2
    margin = jnp.where((source_of == order[0]) | (taker == order[0]) | (lengths[taker] == 0), 0, jnp.maximum(margin, 0))
    passed = jax.random.randint(jax.random.fold_in(own, 4), (number_of // 2,), 0, 1 << 20) % (margin + 1)
    lengths = lengths.at[source_of].add(-passed).at[taker].add(passed)
    items = jnp.searchsorted(jnp.cumsum(lengths), jnp.arange(rows * top), side="right").astype(jnp.int32)
    table = items.reshape(top, rows).T
    table = table[jax.random.permutation(jax.random.fold_in(own, 1), rows)]
    offset_by = jax.random.randint(jax.random.fold_in(own, 2), (rows, 1), 0, top)
    return jnp.take_along_axis(table, (jnp.arange(top)[None, :] + offset_by) % top, axis=1)


def portions_of(amount, total, bound, skew, full):
    portions = [(1 << 20) // math.isqrt(standing ** skew) + 1 for standing in range(1, amount + 1)]
    largest = bound if full else min(bound, max(-(-total // amount), total * portions[0] // sum(portions)))
    least = 1 if total - largest >= amount - 1 else 0
    given, rest = [largest] + [least] * (amount - 1), total - largest - least * (amount - 1)
    while rest > 0:
        free = [i for i in range(1, amount) if given[i] < largest] or [i for i in range(1, amount) if given[i] < bound]
        mass, left = sum([portions[i] for i in free]), rest
        for i in free:
            addition = min(bound - given[i], max(1, left * portions[i] // mass), rest)
            given[i] = given[i] + addition
            rest = rest - addition
    return np.array(given)


def setup_inputs(seed: int = 0) -> dict:
    keys = jax.random.split(jax.random.key(seed), 10)
    estimate = jnp.clip(jnp.exp(math.log(2.0) - 1.3862944 * jax.random.uniform(keys[0], (NX, NY, NZ), jnp.float32) ** block_scale(keys[0], (NX, NY, NZ), ((0, 4), (1, 2)), -0.2, 0.2)), 0.5, 2.0)
    observed = jnp.clip(jnp.exp(math.log(4.0) - 2.7725887 * jax.random.uniform(keys[1], (VIEWS, NB * PIECES, PV), jnp.float32) ** block_scale(keys[1], (VIEWS, NB * PIECES, PV), ((0, 4), (1, 8)), -0.2, 0.2)), 0.25, 4.0)
    destination_keys = jax.random.split(jax.random.fold_in(keys[2], 1), VIEWS * (NB * PIECES) // PIECES)
    destination_turns = jax.random.permutation(jax.random.fold_in(keys[2], 3), VIEWS * (NB * PIECES) // PIECES)
    destination = jax.vmap(lambda own, number: shared_out(jax.random.fold_in(keys[2], 2), own, number, PIECES, NB, 1, CAP, 1))(destination_keys, destination_turns).reshape((VIEWS, NB * PIECES, 1))
    slot_index = place_ends(jax.random.randint(keys[3], (VIEWS, NB * PIECES), 0, SLOTS), jax.random.fold_in(keys[3], 1), 0, SLOTS - 1).astype(jnp.int32)
    valid_count = place_ends(jax.random.randint(keys[4], (VIEWS, NB * PIECES), CZ // 4, CZ + 1), jax.random.fold_in(keys[4], 1), CZ // 4, CZ).astype(jnp.int32)
    blend_weight = jnp.clip(0.2 + 0.8 * jax.random.uniform(keys[5], (VIEWS, NB * PIECES), jnp.float32) ** block_scale(keys[5], (VIEWS, NB * PIECES), ((0, 4), (1, 8)), -0.2, 0.2), 0.2, 1.0)
    kernel_x = jnp.clip(jnp.exp(math.log(1.0) - 2.3025851 * jax.random.uniform(keys[6], (VIEWS, 2 * R + 1), jnp.float32) ** block_scale(keys[6], (VIEWS, 2 * R + 1), ((0, 4),), -0.2, 0.2)), 0.1, 1.0)
    kernel_y = jnp.clip(jnp.exp(math.log(1.0) - 2.3025851 * jax.random.uniform(keys[7], (VIEWS, 2 * R + 1), jnp.float32) ** block_scale(keys[7], (VIEWS, 2 * R + 1), ((0, 4),), -0.2, 0.2)), 0.1, 1.0)
    kernel_z = jnp.clip(jnp.exp(math.log(1.0) - 2.3025851 * jax.random.uniform(keys[8], (VIEWS, 2 * RZ + 1), jnp.float32) ** block_scale(keys[8], (VIEWS, 2 * RZ + 1), ((0, 4),), -0.2, 0.2)), 0.1, 1.0)
    return dict(estimate=estimate, observed=observed, destination=destination, slot_index=slot_index, valid_count=valid_count, blend_weight=blend_weight, kernel_x=kernel_x, kernel_y=kernel_y, kernel_z=kernel_z)


PRIOR_WEIGHT = 0.5


def convolve_axis(volume, kernel, which_axis, radius):
    extent = volume.shape[which_axis]
    widths = [(0, 0), (0, 0), (0, 0)]
    widths[which_axis] = (radius, radius)
    padded = jnp.pad(volume, widths)
    summed = jnp.zeros(volume.shape, jnp.float32)
    for position in range(2 * radius + 1):
        summed = summed + kernel[position] * lax.slice_in_dim(padded, position, position + extent, axis=which_axis)
    return summed


def convolve_all(volume, norm_x, norm_y, norm_z):
    first_pass = convolve_axis(volume, norm_x, 0, R)
    second_pass = convolve_axis(first_pass, norm_y, 1, R)
    return convolve_axis(second_pass, norm_z, 2, RZ)


def to_volume(blocks):
    return blocks.reshape(N_BX, N_BY, CX, CY, CZ).transpose(0, 2, 1, 3, 4).reshape(NX, NY, NZ)


def reference(estimate, observed, destination, slot_index, valid_count, blend_weight, kernel_x, kernel_y, kernel_z):
    logsum = jnp.zeros((NX, NY, NZ), jnp.float32)
    depth_index = jnp.arange(NZ, dtype=jnp.int32)
    for view_number in range(VIEWS):
        norm_x = kernel_x[view_number] / jnp.sum(kernel_x[view_number])
        norm_y = kernel_y[view_number] / jnp.sum(kernel_y[view_number])
        norm_z = kernel_z[view_number] / jnp.sum(kernel_z[view_number])
        blurred = convolve_all(estimate, norm_x, norm_y, norm_z)
        keep_mask = (depth_index[None, :] < valid_count[view_number][:, None]).astype(jnp.float32) * blend_weight[view_number][:, None]
        weighted = (observed[view_number].reshape(-1, YP, CZ) * keep_mask[:, None, :]).reshape(-1, PV)
        target = (destination[view_number, :, 0] * SLOTS + slot_index[view_number]).astype(jnp.int32)
        data_slots = jax.ops.segment_sum(weighted, target, num_segments=NB * SLOTS)
        cover_slots = jax.ops.segment_sum(keep_mask, target, num_segments=NB * SLOTS)
        data_volume = to_volume(data_slots.reshape(NB, CX, CY, CZ))
        cover_wide = jnp.broadcast_to(cover_slots.reshape(NB, CX, CY // YP, 1, CZ), (NB, CX, CY // YP, YP, CZ))
        cover_volume = to_volume(cover_wide.reshape(NB, CX, CY, CZ))
        ratio_field = (data_volume + PRIOR_WEIGHT * blurred) / ((cover_volume + PRIOR_WEIGHT) * blurred)
        correction = convolve_all(ratio_field, norm_x[::-1], norm_y[::-1], norm_z[::-1])
        logsum = logsum + jnp.log(correction)
    return estimate * jnp.exp(logsum)
```

```python
import jax
import jax.numpy as jnp
from jax import lax
from jax.experimental import pallas as pl
from jax.experimental.pallas import tpu as pltpu
from jax.sharding import PartitionSpec as P

R = 8
RZ = 16
YP = 4
PV = 512
SLOTS = 256
PIECES = 256
CX = 64
CY = 16
CZ = 128
PRIOR_WEIGHT = 0.5
F32 = jnp.float32
BF16 = jnp.bfloat16
VM = pl.BlockSpec(memory_space=pltpu.VMEM)
SM = pl.BlockSpec(memory_space=pltpu.SMEM)
GROUP = 64
CHUNK = YP * GROUP + 8


def call(kernel, out_shape, scratch=(), in_specs=None, flops=1 << 22, moved=1 << 20):
    return pl.pallas_call(
        kernel,
        out_shape=[jax.ShapeDtypeStruct(s, F32) for s in out_shape],
        in_specs=in_specs,
        out_specs=[VM] * len(out_shape),
        scratch_shapes=list(scratch),
        compiler_params=pltpu.CompilerParams(vmem_limit_bytes=32 << 20),
        cost_estimate=pl.CostEstimate(flops=flops, bytes_accessed=moved, transcendentals=0),
    )


def three(x):
    high = x.astype(BF16)
    rest = x - high.astype(F32)
    mid = rest.astype(BF16)
    return high, mid, (rest - mid.astype(F32)).astype(BF16)


def two(x):
    high = x.astype(BF16)
    return high, (x - high.astype(F32)).astype(BF16)


def iota(shape, dim):
    return lax.broadcasted_iota(jnp.int32, shape, dim)


def mm(a, b):
    return jnp.dot(a, b, preferred_element_type=F32)


def pack_kernel(observed, target, slot, count, weight, *outs):
    bricks = len(outs)
    me = lax.axis_index("bx") * lax.axis_size("by") + lax.axis_index("by")
    goal = target[...] ^ me
    member = (iota((bricks, PIECES), 0) == goal).astype(F32)
    upto = (iota((PIECES, PIECES), 0) <= iota((PIECES, PIECES), 1)).astype(F32)
    ranks = mm(member.astype(BF16), upto.astype(BF16))
    rank = jnp.sum(member * ranks, axis=0, keepdims=True).astype(jnp.int32) - 1
    place = goal * GROUP + rank
    rows = bricks * GROUP
    pick = (iota((rows, PIECES), 0) == place).astype(F32).astype(BF16)
    keep = jnp.where(iota((CZ, PIECES), 0) < count[...], weight[...], 0.0).T
    weighted = observed[...] * jnp.concatenate([keep] * YP, axis=1)
    packed = sum(mm(pick, part) for part in three(weighted))
    parts = [p.astype(F32) for p in three(weight[...])]
    table = jnp.concatenate(
        [slot[...].astype(F32), count[...].astype(F32)] + parts + [jnp.zeros((3, PIECES), F32)],
        axis=0,
    )
    meta = lax.dot_general(
        table.astype(BF16), pick, (((1,), (1,)), ((), ())), preferred_element_type=F32
    )
    wide = jnp.concatenate(
        [meta[0:2], meta[2:3] + meta[3:4] + meta[4:5], jnp.zeros((5, rows), F32)], axis=0
    )
    lane = iota((8, CZ), 1)
    for s in range(bricks):
        for j in range(YP):
            outs[s][j * GROUP : (j + 1) * GROUP, :] = packed[
                s * GROUP : (s + 1) * GROUP, j * CZ : (j + 1) * CZ
            ]
        pair = wide[:, (s // 2) * CZ : (s // 2 + 1) * CZ]
        if s % 2:
            pair = pltpu.roll(pair, GROUP, 1)
        outs[s][YP * GROUP :, :] = jnp.where(lane < GROUP, pair, 0.0)


def sides():
    odd_x = lax.axis_index("bx") % 2
    odd_y = lax.axis_index("by") % 2
    return odd_x, odd_y


def put_edges(volume, ya, yb, xa, xb):
    odd_x, odd_y = sides()
    ya[...] = volume[pl.ds((1 - odd_y) * (CY - R), R)]
    if yb is not None:
        yb[...] = volume[pl.ds(odd_y * (CY - R), R)]
    xa[...] = volume[:, pl.ds(pl.multiple_of((1 - odd_x) * (CX - R), R), R), :]
    xb[...] = volume[:, pl.ds(pl.multiple_of(odd_x * (CX - R), R), R), :]


def turn_kernel(estimate, turned, ya, *rest):
    for y in range(CY):
        turned[y] = estimate[pl.ds(y, CX, stride=CY), :]
    put_edges(turned, ya, *([None] * (3 - len(rest))), *rest)


def corner_kernel(xa, xb, *outs):
    _, odd_y = sides()
    for phase, out in enumerate(outs):
        start = (odd_y if phase else 1 - odd_y) * (CY - R)
        out[0] = xa[pl.ds(start, R)]
        out[1] = xb[pl.ds(start, R)]


def total(kernel, taps):
    acc = kernel[0, 0]
    for i in range(1, taps):
        acc = acc + kernel[0, i]
    return acc


def spread(own, halos, kx, ky, kz, padded, along_x, along_y, reverse):
    xa, xb, y_sides = halos
    odd_x, odd_y = sides()
    taps, ztaps = 2 * R + 1, 2 * RZ + 1
    xs = [pl.multiple_of((1 - odd_x) * (CX + R), R), pl.multiple_of(odd_x * (CX + R), R)]
    ys = [(1 - odd_y) * (CY + R), odd_y * (CY + R)]
    padded[R : R + CY, R : R + CX, :] = own[...]
    padded[R : R + CY, pl.ds(xs[0], R), :] = xa[...]
    padded[R : R + CY, pl.ds(xs[1], R), :] = xb[...]
    for phase in range(2):
        rows = pl.ds(ys[phase], R)
        if phase < len(y_sides):
            edge, corner = y_sides[phase]
            padded[rows, R : R + CX, :] = edge[...]
            padded[rows, pl.ds(xs[0], R), :] = corner[0]
            padded[rows, pl.ds(xs[1], R), :] = corner[1]
        else:
            padded[rows] = jnp.zeros((R, CX + 2 * R, CZ), F32)

    def tap(kernel, n, i):
        return kernel[0, n - 1 - i] if reverse else kernel[0, i]

    wide = 3 * (CX + 2 * R)
    col, row = iota((CX, wide), 1), iota((CX, wide), 0)
    block = col // (CX + 2 * R)
    gap = col - block * (CX + 2 * R) - row
    band = jnp.zeros((CX, wide), F32)
    for i in range(taps):
        band = jnp.where(gap == i, tap(kx, taps, i), band)
    band = band / total(kx, taps)
    high, low = two(band)
    band_x = jnp.where(block == 1, low.astype(F32), high.astype(F32)).astype(BF16)

    gap = iota((CZ, CZ), 0) - iota((CZ, CZ), 1) + RZ
    band = jnp.zeros((CZ, CZ), F32)
    for i in range(ztaps):
        band = jnp.where(gap == i, tap(kz, ztaps, i), band)
    band = band / total(kz, ztaps) / total(ky, taps)
    high, low = two(band)
    band_z = jnp.concatenate([high, low, high], axis=0)

    for y in range(0, CY + 2 * R, 2):
        stack = []
        for k in range(2):
            high, low = two(padded[y + k])
            stack.append(jnp.concatenate([high, high, low], axis=0))
        both = mm(band_x, jnp.concatenate(stack, axis=1))
        along_x[y] = both[:, :CZ]
        along_x[y + 1] = both[:, CZ:]

    def tile(t, carry):
        at = pl.ds(pl.multiple_of(t * 8, 8), 8)
        acc = [None] * CY
        for i in range(CY + 2 * R):
            value = along_x[i, at, :]
            for y in range(CY):
                if 0 <= i - y < taps:
                    term = tap(ky, taps, i - y) * value
                    acc[y] = term if acc[y] is None else acc[y] + term
        for y in range(CY):
            along_y[y, at, :] = acc[y]
        return carry

    lax.fori_loop(0, CX // 8, tile, 0)
    out = []
    for y in range(0, CY, 4):
        block = along_y[y : y + 4].reshape(4 * CX, CZ)
        high, low = two(block)
        result = mm(jnp.concatenate([high, high, low], axis=1), band_z)
        out += [result[k * CX : (k + 1) * CX] for k in range(4)]
    return out


def split_halos(refs, phases):
    own, xa, xb = refs[:3]
    y_sides = [(refs[3 + 2 * p], refs[4 + 2 * p]) for p in range(phases)]
    return own, (xa, xb, y_sides), refs[3 + 2 * phases :]


def blur_kernel(phases, *refs):
    own, halos, (kx, ky, kz, out, padded, along_x, along_y) = split_halos(refs, phases)
    for y, value in enumerate(spread(own, halos, kx, ky, kz, padded, along_x, along_y, False)):
        out[y] = value


def correct_kernel(phases, *refs):
    own, halos, (kx, ky, kz, mine, other, padded, along_x, along_y) = split_halos(refs, phases)
    values = spread(own, halos, kx, ky, kz, padded, along_x, along_y, True)
    core = lax.axis_index("view") % 2
    half = CY // 2
    for low, high in ((0, 1), (1, 0)):

        @pl.when(core == low)
        def _():
            for y in range(half):
                mine[y] = values[low * half + y]
                other[y] = values[high * half + y]


def ratio_kernel(chunks, *refs):
    parts, blurred = refs[:chunks], refs[chunks]
    ratio, ya, *rest = refs[chunks + 1 :]
    rows = chunks * GROUP
    metas = []
    for c in range(0, chunks, 2):
        odd = pltpu.roll(parts[c + 1][YP * GROUP :, :], GROUP, 1)
        metas.append(parts[c][YP * GROUP :, :] + odd)
    meta = jnp.concatenate(metas, axis=1)
    slot, count, weight = meta[0:1].astype(jnp.int32), meta[1:2].astype(jnp.int32), meta[2:3]
    key = (slot & (YP - 1)) * CX + (slot >> 2)
    chooser = (iota((SLOTS, rows), 0) == key).astype(F32).astype(BF16)
    keep = jnp.where(iota((CZ, rows), 0) < count, weight, 0.0).T

    def gathered(values):
        return sum(mm(chooser, part) for part in three(values))

    cover = gathered(keep)
    for j in range(0, YP, 2):
        values = jnp.concatenate(
            [
                jnp.concatenate([p[k * GROUP : (k + 1) * GROUP, :] for p in parts], axis=0)
                for k in (j, j + 1)
            ],
            axis=1,
        )
        data = gathered(values)
        for q in range(CY // YP):
            at = slice(q * CX, (q + 1) * CX)
            for k in range(2):
                y = YP * q + j + k
                base = blurred[y]
                ratio[y] = (data[at, k * CZ : (k + 1) * CZ] + PRIOR_WEIGHT * base) / (
                    (cover[at] + PRIOR_WEIGHT) * base
                )
    put_edges(ratio, ya, *([None] * (3 - len(rest))), *rest)


def finish_kernel(mine, other, estimate, out):
    core = lax.axis_index("view") % 2
    half = CY // 2
    for low in range(2):

        @pl.when(core == low)
        def _():
            for y in range(CY):
                source = mine if y // half == low else other
                rows = pl.ds(y, CX, stride=CY)
                out[rows, :] = source[y % half] * estimate[rows, :]


def swap(x, axis, mask):
    return lax.ppermute(x, axis, [(i, i ^ mask) for i in range(lax.axis_size(axis))])


def pairs(axis):
    count = lax.axis_size(axis)
    first = [(i, i ^ 1) for i in range(count) if i ^ 1 < count]
    second = [(i, ((i + 1) ^ 1) - 1) for i in range(count)]
    second = [(i, k) for i, k in second if 0 <= k < count]
    return [first] + ([second] if second else [])


def halo(edges, y_phases):
    y_edges, xa, xb = edges[:y_phases], edges[-2], edges[-1]
    x_pairs, y_pairs = pairs("bx"), pairs("by")
    y_got = [lax.ppermute(e, "by", pair) for e, pair in zip(y_edges, y_pairs)]
    xa = lax.ppermute(xa, "bx", x_pairs[0])
    xb = lax.ppermute(xb, "bx", x_pairs[1]) if len(x_pairs) > 1 else jnp.zeros_like(xb)
    corners = call(corner_kernel, [(2, R, R, CZ)] * y_phases, in_specs=[VM] * 2)(xa, xb)
    c_got = [lax.ppermute(c, "by", pair) for c, pair in zip(corners, y_pairs)]
    out = [xa, xb]
    for edge, corner in zip(y_got, c_got):
        out += [edge, corner]
    return out


def generic_exchange(bricks, observed, target, slot, count, weight):
    capacity = max(4, 2 * PIECES // bricks)
    member = (target[:, None] == jnp.arange(bricks)[None, :]).astype(jnp.int32)
    slot_rank = jnp.sum((jnp.cumsum(member, axis=0) - 1) * member, axis=1)
    place = target * capacity + slot_rank
    keep = jnp.where(jnp.arange(CZ)[None, :] < count[:, None], weight[:, None], 0.0)
    weighted = (observed.reshape(-1, YP, CZ) * keep[:, None, :]).reshape(-1, PV)
    facts = jnp.stack([slot.astype(F32), count.astype(F32), weight], axis=1)
    rows = jnp.zeros((bricks * capacity, PV), F32).at[place].set(weighted)
    facts = jnp.zeros((bricks * capacity, 3), F32).at[place].set(facts)

    def exchange(x):
        x = x.reshape(bricks, capacity, -1)
        return lax.all_to_all(x, ("bx", "by"), split_axis=0, concat_axis=0, tiled=True)

    chunks = bricks * capacity // GROUP
    rows = exchange(rows).reshape(chunks, GROUP, YP, CZ).transpose(0, 2, 1, 3)
    facts = exchange(facts).reshape(chunks, GROUP, 3).transpose(0, 2, 1)
    facts = jnp.pad(facts, ((0, 0), (0, 5), (0, CZ - GROUP)))
    both = jnp.concatenate([rows.reshape(chunks, YP * GROUP, CZ), facts], axis=1)
    return [both[c] for c in range(chunks)]


def local(
    estimate,
    observed,
    destination,
    slot_index,
    valid_count,
    blend_weight,
    kernel_x,
    kernel_y,
    kernel_z,
):
    count_bx, count_by = lax.axis_size("bx"), lax.axis_size("by")
    bricks = count_bx * count_by
    y_phases = len(pairs("by"))
    flat = estimate.reshape(CX * CY, CZ)
    edge_shapes = [(R, CX, CZ)] * y_phases + [(CY, R, CZ)] * 2
    brick = (CY, CX, CZ)
    half = (CY // 2, CX, CZ)
    kernels = (kernel_x, kernel_y, kernel_z)
    work = [
        pltpu.VMEM((CY + 2 * R, CX + 2 * R, CZ), F32),
        pltpu.VMEM((CY + 2 * R, CX, CZ), F32),
        pltpu.VMEM(brick, F32),
    ]
    halo_specs = [VM] * (3 + 2 * y_phases) + [SM] * 3

    if bricks * GROUP == 2 * PIECES:
        packed = call(pack_kernel, [(CHUNK, CZ)] * bricks, in_specs=[VM] * 5)(
            observed[0], destination.reshape(1, PIECES), slot_index, valid_count, blend_weight
        )
        chunks = [packed[0]]
        for s in sorted(range(1, bricks), reverse=True):
            pair = [(d, d ^ s) for d in range(bricks)]
            chunks.append(lax.ppermute(packed[s], ("bx", "by"), pair))
    else:
        chunks = generic_exchange(
            bricks,
            observed[0],
            destination[0, :, 0],
            slot_index[0],
            valid_count[0],
            blend_weight[0],
        )

    turned, *edges = call(turn_kernel, [brick] + edge_shapes, in_specs=[VM])(flat)
    around = halo(edges, y_phases)

    def blur(*refs):
        blur_kernel(y_phases, *refs)

    (blurred,) = call(blur, [brick], work, halo_specs)(turned, *around, *kernels)

    def ratios(*refs):
        ratio_kernel(len(chunks), *refs)

    ratio, *edges = call(
        ratios, [brick] + edge_shapes, in_specs=[VM] * (len(chunks) + 1)
    )(*chunks, blurred)
    around = halo(edges, y_phases)

    def correct(*refs):
        correct_kernel(y_phases, *refs)

    mine, other = call(correct, [half, half], work, halo_specs)(ratio, *around, *kernels)
    mine = mine * swap(other, "view", 1)
    mine = mine * swap(mine, "view", 2)
    other = swap(mine, "view", 1)
    (updated,) = call(finish_kernel, [(CX * CY, CZ)], in_specs=[VM] * 3)(mine, other, flat)
    return updated.reshape(CX, CY, CZ)


def solution(mesh):
    placed = (
        P("bx", "by", None),
        P("view", ("bx", "by"), None),
        P("view", ("bx", "by"), None),
        P("view", ("bx", "by")),
        P("view", ("bx", "by")),
        P("view", ("bx", "by")),
        P("view", None),
        P("view", None),
        P("view", None),
    )
    return jax.shard_map(
        local, mesh=mesh, in_specs=placed, out_specs=P("bx", "by", None), check_vma=False
    )
```

```python
import jax
import jax.numpy as jnp
from jax import lax
from jax.experimental import pallas as pl
from jax.experimental.pallas import tpu as pltpu
from jax.sharding import PartitionSpec as P

R = 8
RZ = 16
YP = 4
PV = 512
SLOTS = 256
PIECES = 256
CX = 64
CY = 16
CZ = 128
PRIOR_WEIGHT = 0.5
F32 = jnp.float32
BF16 = jnp.bfloat16
VM = pl.BlockSpec(memory_space=pltpu.VMEM)
SM = pl.BlockSpec(memory_space=pltpu.SMEM)
ANY = pl.BlockSpec(memory_space=pl.ANY)
HB = pl.BlockSpec(memory_space=pltpu.HBM)
HX = CX // 2
HE = HX + 2 * R
GROUP = 64
CHUNK = YP * GROUP + 8


def call(
    kernel,
    outs,
    scratch=(),
    in_specs=None,
    out_specs=None,
    aliases=None,
    flops=1 << 22,
    moved=1 << 20,
):
    shapes = [o if hasattr(o, "dtype") else jax.ShapeDtypeStruct(o, F32) for o in outs]
    return pl.pallas_call(
        kernel,
        out_shape=shapes,
        in_specs=in_specs,
        out_specs=out_specs or [VM] * len(outs),
        scratch_shapes=list(scratch),
        input_output_aliases=aliases or {},
        compiler_params=pltpu.CompilerParams(vmem_limit_bytes=32 << 20),
        cost_estimate=pl.CostEstimate(flops=flops, bytes_accessed=moved, transcendentals=0),
    )


def three(x):
    high = x.astype(BF16)
    rest = x - high.astype(F32)
    mid = rest.astype(BF16)
    return high, mid, (rest - mid.astype(F32)).astype(BF16)


def two(x):
    high = x.astype(BF16)
    return high, (x - high.astype(F32)).astype(BF16)


def iota(shape, dim):
    return lax.broadcasted_iota(jnp.int32, shape, dim)


def mm(a, b):
    return jnp.dot(a, b, preferred_element_type=F32)


def pack_kernel(*refs):
    sources, outs, held, sems = refs[:5], refs[5:-6], refs[-6:-1], refs[-1]
    bricks = len(outs)
    copies = [
        pltpu.make_async_copy(source, to, sems.at[i])
        for i, (source, to) in enumerate(zip(sources, held))
    ]
    for copy in copies:
        copy.start()
    observed, target, slot, count, weight = held
    for copy in copies[1:]:
        copy.wait()
    me = lax.axis_index("bx") * lax.axis_size("by") + lax.axis_index("by")
    goal = target[...] ^ me
    member = (iota((bricks, PIECES), 0) == goal).astype(F32)
    upto = (iota((PIECES, PIECES), 0) <= iota((PIECES, PIECES), 1)).astype(F32)
    ranks = mm(member.astype(BF16), upto.astype(BF16))
    rank = jnp.sum(member * ranks, axis=0, keepdims=True).astype(jnp.int32) - 1
    place = goal * GROUP + rank
    rows = bricks * GROUP
    pick = (iota((rows, PIECES), 0) == place).astype(F32).astype(BF16)
    keep = jnp.where(iota((CZ, PIECES), 0) < count[...], weight[...], 0.0).T
    copies[0].wait()
    weighted = observed[...] * jnp.concatenate([keep] * YP, axis=1)
    packed = sum(mm(pick, part) for part in three(weighted))
    parts = [p.astype(F32) for p in three(weight[...])]
    table = jnp.concatenate(
        [slot[...].astype(F32), count[...].astype(F32)] + parts + [jnp.zeros((3, PIECES), F32)],
        axis=0,
    )
    meta = lax.dot_general(
        table.astype(BF16), pick, (((1,), (1,)), ((), ())), preferred_element_type=F32
    )
    wide = jnp.concatenate(
        [meta[0:2], meta[2:3] + meta[3:4] + meta[4:5], jnp.zeros((5, rows), F32)], axis=0
    )
    lane = iota((8, CZ), 1)
    for s in range(bricks):
        for j in range(YP):
            outs[s][j * GROUP : (j + 1) * GROUP, :] = packed[
                s * GROUP : (s + 1) * GROUP, j * CZ : (j + 1) * CZ
            ]
        pair = wide[:, (s // 2) * CZ : (s // 2 + 1) * CZ]
        if s % 2:
            pair = pltpu.roll(pair, GROUP, 1)
        outs[s][YP * GROUP :, :] = jnp.where(lane < GROUP, pair, 0.0)


def sides():
    odd_x = lax.axis_index("bx") % 2
    odd_y = lax.axis_index("by") % 2
    return odd_x, odd_y


def put_edges(volume, outs):
    odd_x, odd_y = sides()
    at_x = [pl.multiple_of((1 - odd_x) * (CX - R), R), pl.multiple_of(odd_x * (CX - R), R)]
    at_y = [(1 - odd_y) * (CY - R), odd_y * (CY - R)]
    for phase in range((len(outs) - 2) // 3):
        whole, first, second = outs[3 * phase : 3 * phase + 3]
        rows = pl.ds(at_y[phase], R)
        whole[...] = volume[rows]
        first[...] = volume[rows, pl.ds(at_x[0], R), :]
        second[...] = volume[rows, pl.ds(at_x[1], R), :]
    outs[-2][...] = volume[:, pl.ds(at_x[0], R), :]
    outs[-1][...] = volume[:, pl.ds(at_x[1], R), :]


def put_halos(own, halos, padded):
    odd_x, odd_y = sides()
    at_x = [pl.multiple_of((1 - odd_x) * (CX + R), R), pl.multiple_of(odd_x * (CX + R), R)]
    at_y = [(1 - odd_y) * (CY + R), odd_y * (CY + R)]
    padded[R : R + CY, R : R + CX, :] = own[...]
    for phase in range((len(halos) - 2) // 3):
        whole, first, second = halos[3 * phase : 3 * phase + 3]
        rows = pl.ds(at_y[phase], R)
        padded[rows, R : R + CX, :] = whole[...]
        padded[rows, pl.ds(at_x[0], R), :] = first[...]
        padded[rows, pl.ds(at_x[1], R), :] = second[...]
    padded[R : R + CY, pl.ds(at_x[0], R), :] = halos[-2][...]
    padded[R : R + CY, pl.ds(at_x[1], R), :] = halos[-1][...]


def turn_kernel(estimate, turned, *edges):
    for y in range(CY):
        turned[y] = estimate[pl.ds(y, CX, stride=CY), :]
    put_edges(turned, edges)


def total(kernel, taps):
    acc = kernel[0, 0]
    for i in range(1, taps):
        acc = acc + kernel[0, i]
    return acc


def band_kernel(kx, ky, kz, *outs):
    taps, ztaps = 2 * R + 1, 2 * RZ + 1
    for reverse in range(2):
        col, row = iota((HX, 3 * HE), 1), iota((HX, 3 * HE), 0)
        block = col // HE
        gap = col - block * HE - row
        band = jnp.zeros((HX, 3 * HE), F32)
        for i in range(taps):
            band = jnp.where(gap == i, kx[0, taps - 1 - i if reverse else i], band)
        high, low = two(band / total(kx, taps))
        middle = jnp.where(block == 1, low.astype(F32), high.astype(F32))
        outs[2 * reverse][...] = middle.astype(BF16)
        gap = iota((CZ, CZ), 0) - iota((CZ, CZ), 1) + RZ
        band = jnp.zeros((CZ, CZ), F32)
        for i in range(ztaps):
            band = jnp.where(gap == i, kz[0, ztaps - 1 - i if reverse else i], band)
        high, low = two(band / total(kz, ztaps) / total(ky, taps))
        outs[2 * reverse + 1][...] = jnp.concatenate([high, low, high], axis=0)


def spread(padded, start, ky, band_x, band_z, along_x, along_y, phases, reverse):
    taps = 2 * R + 1
    tap = [ky[0, taps - 1 - i if reverse else i] for i in range(taps)]
    lines, base = CY + 2 * R, 0
    if phases == 1:
        odd_y = lax.axis_index("by") % 2
        lines, base = CY + R, R * (1 - odd_y)
        along_x[pl.ds((CY + R) * odd_y, R)] = jnp.zeros((R, HX, CZ), F32)
    first = pl.ds(pl.multiple_of(start, HX), HE)
    for y in range(0, lines, 2):
        stack = []
        for k in range(2):
            high, low = two(padded[base + y + k, first, :])
            stack.append(jnp.concatenate([high, high, low], axis=0))
        both = mm(band_x[...], jnp.concatenate(stack, axis=1))
        along_x[base + y] = both[:, :CZ]
        along_x[base + y + 1] = both[:, CZ:]

    def tile(t, carry):
        at = pl.ds(pl.multiple_of(t * 8, 8), 8)
        acc = [None] * CY
        for i in range(CY + 2 * R):
            value = along_x[i, at, :]
            for y in range(CY):
                if 0 <= i - y < taps:
                    term = tap[i - y] * value
                    acc[y] = term if acc[y] is None else acc[y] + term
        for y in range(CY):
            along_y[y, at, :] = acc[y]
        return carry

    lax.fori_loop(0, HX // 8, tile, 0)
    out = []
    for y in range(0, CY, 8):
        high, low = two(along_y[y : y + 8].reshape(8 * HX, CZ))
        result = mm(jnp.concatenate([high, high, low], axis=1), band_z[...])
        out += [result[k * HX : (k + 1) * HX] for k in range(8)]
    return out


def blur_kernel(phases, own, *refs):
    halos, (ky, band_x, band_z, out, padded, along_x, along_y) = refs[:-7], refs[-7:]
    put_halos(own, halos, padded)
    for start in range(0, CX, HX):
        values = spread(padded, start, ky, band_x, band_z, along_x, along_y, phases, False)
        for y in range(CY):
            out[y, start : start + HX, :] = values[y]


def correct_half(phases, part, padded, ky, band_x, band_z, out, along_x, along_y):
    values = spread(padded, HX * part, ky, band_x, band_z, along_x, along_y, phases, True)
    for y in range(CY):
        out[pl.ds(y, HX, stride=CY), :] = values[y]


def first_kernel(phases, own, *refs):
    halos, (ky, band_x, band_z, out, padded, along_x, along_y) = refs[:-7], refs[-7:]
    put_halos(own, halos, padded)
    part = 1 - lax.axis_index("view") % 2
    correct_half(phases, part, padded, ky, band_x, band_z, out, along_x, along_y)


def second_kernel(phases, padded, ky, band_x, band_z, out, along_x, along_y):
    part = lax.axis_index("view") % 2
    correct_half(phases, part, padded, ky, band_x, band_z, out, along_x, along_y)


def ratio_kernel(chunks, *refs):
    parts, blurred = refs[:chunks], refs[chunks]
    ratio, *edges = refs[chunks + 1 :]
    rows = chunks * GROUP
    metas = []
    for c in range(0, chunks, 2):
        odd = pltpu.roll(parts[c + 1][YP * GROUP :, :], GROUP, 1)
        metas.append(parts[c][YP * GROUP :, :] + odd)
    meta = jnp.concatenate(metas, axis=1)
    slot, count, weight = meta[0:1].astype(jnp.int32), meta[1:2].astype(jnp.int32), meta[2:3]
    key = (slot & (YP - 1)) * CX + (slot >> 2)
    chooser = (iota((SLOTS, rows), 0) == key).astype(F32).astype(BF16)
    keep = jnp.where(iota((CZ, rows), 0) < count, weight, 0.0).T

    def gathered(values):
        return sum(mm(chooser, part) for part in three(values))

    cover = gathered(keep)
    for j in range(0, YP, 2):
        values = jnp.concatenate(
            [
                jnp.concatenate([p[k * GROUP : (k + 1) * GROUP, :] for p in parts], axis=0)
                for k in (j, j + 1)
            ],
            axis=1,
        )
        data = gathered(values)
        for q in range(CY // YP):
            at = slice(q * CX, (q + 1) * CX)
            for k in range(2):
                y = YP * q + j + k
                base = blurred[y]
                ratio[y] = (data[at, k * CZ : (k + 1) * CZ] + PRIOR_WEIGHT * base) / (
                    (cover[at] + PRIOR_WEIGHT) * base
                )
    put_edges(ratio, edges)


def store_kernel(mine, part, *refs):
    out, sem = refs[-2:]
    half = HX * CY
    start = pl.multiple_of(half * ((lax.axis_index("view") + part) % 2), half)
    copy = pltpu.make_async_copy(mine, out.at[pl.ds(start, half), :], sem)
    copy.start()
    copy.wait()


def swap(x, axis, mask):
    return lax.ppermute(x, axis, [(i, i ^ mask) for i in range(lax.axis_size(axis))])


def pairs(axis):
    count = lax.axis_size(axis)
    first = [(i, i ^ 1) for i in range(count) if i ^ 1 < count]
    second = [(i, ((i + 1) ^ 1) - 1) for i in range(count)]
    second = [(i, k) for i, k in second if 0 <= k < count]
    return [first] + ([second] if second else [])


def halo_pairs():
    x_pairs, y_pairs, wide = pairs("bx"), pairs("by"), lax.axis_size("by")
    x_pairs = x_pairs + [[]] * (2 - len(x_pairs))
    out = []
    for ys in y_pairs:
        out.append(("by", ys))
        for xs in x_pairs:
            moves = [(a * wide + c, b * wide + d) for a, b in xs for c, d in ys]
            out.append((("bx", "by"), moves))
    return out + [("bx", xs) for xs in x_pairs]


def halo(edges):
    got = []
    for edge, (axis, moves) in zip(edges, halo_pairs()):
        got.append(lax.ppermute(edge, axis, moves) if moves else jnp.zeros_like(edge))
    return got


def generic_exchange(bricks, observed, target, slot, count, weight):
    capacity = max(4, 2 * PIECES // bricks)
    member = (target[:, None] == jnp.arange(bricks)[None, :]).astype(jnp.int32)
    slot_rank = jnp.sum((jnp.cumsum(member, axis=0) - 1) * member, axis=1)
    place = target * capacity + slot_rank
    keep = jnp.where(jnp.arange(CZ)[None, :] < count[:, None], weight[:, None], 0.0)
    weighted = (observed.reshape(-1, YP, CZ) * keep[:, None, :]).reshape(-1, PV)
    facts = jnp.stack([slot.astype(F32), count.astype(F32), weight], axis=1)
    rows = jnp.zeros((bricks * capacity, PV), F32).at[place].set(weighted)
    facts = jnp.zeros((bricks * capacity, 3), F32).at[place].set(facts)

    def exchange(x):
        x = x.reshape(bricks, capacity, -1)
        return lax.all_to_all(x, ("bx", "by"), split_axis=0, concat_axis=0, tiled=True)

    chunks = bricks * capacity // GROUP
    rows = exchange(rows).reshape(chunks, GROUP, YP, CZ).transpose(0, 2, 1, 3)
    facts = exchange(facts).reshape(chunks, GROUP, 3).transpose(0, 2, 1)
    facts = jnp.pad(facts, ((0, 0), (0, 5), (0, CZ - GROUP)))
    both = jnp.concatenate([rows.reshape(chunks, YP * GROUP, CZ), facts], axis=1)
    return [both[c] for c in range(chunks)]


def local(
    estimate,
    observed,
    destination,
    slot_index,
    valid_count,
    blend_weight,
    kernel_x,
    kernel_y,
    kernel_z,
):
    count_bx, count_by = lax.axis_size("bx"), lax.axis_size("by")
    bricks = count_bx * count_by
    phases = len(pairs("by"))
    flat = estimate.reshape(CX * CY, CZ)
    edge_shapes = [(R, CX, CZ), (R, R, CZ), (R, R, CZ)] * phases + [(CY, R, CZ)] * 2
    brick, half = (CY, CX, CZ), (CY * HX, CZ)
    around = (CY + 2 * R, CX + 2 * R, CZ)
    work = [pltpu.VMEM((CY + 2 * R, HX, CZ), F32), pltpu.VMEM((CY, HX, CZ), F32)]
    halo_specs = [VM] * (3 + 3 * phases) + [SM, VM, VM]

    if bricks * GROUP == 2 * PIECES:
        held = [pltpu.VMEM((PIECES, PV), F32)]
        held += [pltpu.VMEM((1, PIECES), jnp.int32)] * 3 + [pltpu.VMEM((1, PIECES), F32)]
        held.append(pltpu.SemaphoreType.DMA((5,)))
        packed = call(pack_kernel, [(CHUNK, CZ)] * bricks, held, [HB] * 5)(
            observed[0], destination.reshape(1, PIECES), slot_index, valid_count, blend_weight
        )
        chunks = [packed[0]]
        for s in sorted(range(1, bricks), reverse=True):
            pair = [(d, d ^ s) for d in range(bricks)]
            chunks.append(lax.ppermute(packed[s], ("bx", "by"), pair))
    else:
        chunks = generic_exchange(
            bricks,
            observed[0],
            destination[0, :, 0],
            slot_index[0],
            valid_count[0],
            blend_weight[0],
        )

    flat, chunks[0] = lax.optimization_barrier((flat, chunks[0]))
    turned, *edges = call(turn_kernel, [brick] + edge_shapes, in_specs=[VM])(flat)
    shapes = [(HX, 3 * HE), (3 * CZ, CZ)] * 2
    bands = call(
        band_kernel, [jax.ShapeDtypeStruct(shape, BF16) for shape in shapes], in_specs=[SM] * 3
    )(kernel_x, kernel_y, kernel_z)

    def blur(*refs):
        blur_kernel(phases, *refs)

    (blurred,) = call(blur, [brick], [pltpu.VMEM(around, F32)] + work, halo_specs)(
        turned, *halo(edges), kernel_y, *bands[:2]
    )

    def ratios(*refs):
        ratio_kernel(len(chunks), *refs)

    ratio, *edges = call(ratios, [brick] + edge_shapes, in_specs=[VM] * (len(chunks) + 1))(
        *chunks, blurred
    )

    def first(*refs):
        first_kernel(phases, *refs)

    def second(*refs):
        second_kernel(phases, *refs)

    other, padded = call(first, [half, around], work, halo_specs)(
        ratio, *halo(edges), kernel_y, *bands[2:]
    )
    (mine,) = call(second, [half], work, [VM, SM, VM, VM])(padded, kernel_y, *bands[2:])
    mine = mine * swap(other, "view", 1)
    own = lax.dynamic_slice_in_dim(flat, lax.axis_index("view") % 2 * half[0], half[0], 0)
    mine = mine * swap(mine, "view", 2) * own

    def store_mine(mine, out, sem):
        store_kernel(mine, 0, out, sem)

    def store_other(other, before, out, sem):
        store_kernel(other, 1, out, sem)

    sem = [pltpu.SemaphoreType.DMA]
    whole = [(CX * CY, CZ)]
    (updated,) = call(store_mine, whole, sem, [VM], [ANY])(mine)
    other = swap(mine, "view", 1)
    (updated,) = call(store_other, whole, sem, [VM, ANY], [ANY], {1: 0})(other, updated)
    return updated.reshape(CX, CY, CZ)


def solution(mesh):
    placed = (
        P("bx", "by", None),
        P("view", ("bx", "by"), None),
        P("view", ("bx", "by"), None),
        P("view", ("bx", "by")),
        P("view", ("bx", "by")),
        P("view", ("bx", "by")),
        P("view", None),
        P("view", None),
        P("view", None),
    )
    return jax.shard_map(
        local, mesh=mesh, in_specs=placed, out_specs=P("bx", "by", None), check_vma=False
    )
```

```python
import jax
import jax.numpy as jnp
from jax import lax
from jax.experimental import pallas as pl
from jax.experimental.pallas import tpu as pltpu
from jax.sharding import PartitionSpec as P


R = 8
RZ = 16
YP = 4
PV = 512
SLOTS = 256
PIECES = 256
CX = 64
CY = 16
CZ = 128
PRIOR_WEIGHT = 0.5
F32 = jnp.float32
BF16 = jnp.bfloat16
VM = pl.BlockSpec(memory_space=pltpu.VMEM)
SM = pl.BlockSpec(memory_space=pltpu.SMEM)
ANY = pl.BlockSpec(memory_space=pl.ANY)
HB = pl.BlockSpec(memory_space=pltpu.HBM)
HX = CX // 2
HY = CY // 2
XE = CX + 2 * R
TAPS = 2 * R + 1
ROWS = 24
PACK_LIMIT = 32 << 20
BLUR_LIMIT = 32 << 20
GROUP = 64
CHUNK = YP * GROUP + 8


def call(
    kernel,
    outs,
    scratch=(),
    in_specs=None,
    out_specs=None,
    aliases=None,
    limit=32 << 20,
    flops=1 << 22,
    moved=1 << 20,
):
    shapes = [o if hasattr(o, "dtype") else jax.ShapeDtypeStruct(o, F32) for o in outs]
    return pl.pallas_call(
        kernel,
        out_shape=shapes,
        in_specs=in_specs,
        out_specs=out_specs or [VM] * len(outs),
        scratch_shapes=list(scratch),
        input_output_aliases=aliases or {},
        compiler_params=pltpu.CompilerParams(vmem_limit_bytes=limit),
        cost_estimate=pl.CostEstimate(flops=flops, bytes_accessed=moved, transcendentals=0),
    )


def three(x):
    high = x.astype(BF16)
    rest = x - high.astype(F32)
    mid = rest.astype(BF16)
    return high, mid, (rest - mid.astype(F32)).astype(BF16)


def two(x):
    high = x.astype(BF16)
    return high, (x - high.astype(F32)).astype(BF16)


def iota(shape, dim):
    return lax.broadcasted_iota(jnp.int32, shape, dim)


def mm(a, b):
    return jnp.dot(a, b, preferred_element_type=F32)


def pack_kernel(*refs):
    sources, outs, token, held, sems = refs[:5], refs[5:-7], refs[-7], refs[-6:-1], refs[-1]
    bricks = len(outs)
    token[...] = jnp.zeros((8, CZ), F32)
    copies = [
        pltpu.make_async_copy(source, to, sems.at[i])
        for i, (source, to) in enumerate(zip(sources, held))
    ]
    for copy in copies:
        copy.start()
    observed, target, slot, count, weight = held
    for copy in copies[1:]:
        copy.wait()
    me = lax.axis_index("bx") * lax.axis_size("by") + lax.axis_index("by")
    goal = target[...] ^ me
    member = (iota((bricks, PIECES), 0) == goal).astype(F32)
    upto = (iota((PIECES, PIECES), 0) <= iota((PIECES, PIECES), 1)).astype(F32)
    ranks = mm(member.astype(BF16), upto.astype(BF16))
    rank = jnp.sum(member * ranks, axis=0, keepdims=True).astype(jnp.int32) - 1
    place = goal * GROUP + rank
    rows = bricks * GROUP
    pick = (iota((rows, PIECES), 0) == place).astype(F32).astype(BF16)
    keep = jnp.where(iota((CZ, PIECES), 0) < count[...], weight[...], 0.0).T
    copies[0].wait()
    weighted = observed[...] * jnp.concatenate([keep] * YP, axis=1)
    packed = sum(mm(pick, part) for part in three(weighted))
    parts = [p.astype(F32) for p in three(weight[...])]
    table = jnp.concatenate(
        [slot[...].astype(F32), count[...].astype(F32)] + parts + [jnp.zeros((3, PIECES), F32)],
        axis=0,
    )
    meta = lax.dot_general(
        table.astype(BF16), pick, (((1,), (1,)), ((), ())), preferred_element_type=F32
    )
    wide = jnp.concatenate(
        [meta[0:2], meta[2:3] + meta[3:4] + meta[4:5], jnp.zeros((5, rows), F32)], axis=0
    )
    lane = iota((8, CZ), 1)
    for s in range(bricks):
        for j in range(YP):
            outs[s][j * GROUP : (j + 1) * GROUP, :] = packed[
                s * GROUP : (s + 1) * GROUP, j * CZ : (j + 1) * CZ
            ]
        pair = wide[:, (s // 2) * CZ : (s // 2 + 1) * CZ]
        if s % 2:
            pair = pltpu.roll(pair, GROUP, 1)
        outs[s][YP * GROUP :, :] = jnp.where(lane < GROUP, pair, 0.0)


def sides():
    odd_x = lax.axis_index("bx") % 2
    odd_y = lax.axis_index("by") % 2
    return odd_x, odd_y


def put_edges(volume, outs):
    odd_x, odd_y = sides()
    at_x = [pl.multiple_of((1 - odd_x) * (CX - R), R), pl.multiple_of(odd_x * (CX - R), R)]
    at_y = [(1 - odd_y) * (CY - R), odd_y * (CY - R)]
    for phase in range((len(outs) - 2) // 3):
        whole, first, second = outs[3 * phase : 3 * phase + 3]
        rows = pl.ds(at_y[phase], R)
        whole[...] = volume[rows]
        first[...] = volume[rows, pl.ds(at_x[0], R), :]
        second[...] = volume[rows, pl.ds(at_x[1], R), :]
    outs[-2][...] = volume[:, pl.ds(at_x[0], R), :]
    outs[-1][...] = volume[:, pl.ds(at_x[1], R), :]


def turn_kernel(estimate, after, turned, *edges):
    for y in range(CY):
        turned[y] = estimate[pl.ds(y, CX, stride=CY), :]
    put_edges(turned, edges)


def total(kernel, taps):
    acc = kernel[0, 0]
    for i in range(1, taps):
        acc = acc + kernel[0, i]
    return acc


def make_bands(kx, ky, kz, *outs):
    ztaps = 2 * RZ + 1
    for reverse in range(2):
        band_x, band_z, taps = outs[3 * reverse : 3 * reverse + 3]
        col, row = iota((CX, 3 * XE), 1), iota((CX, 3 * XE), 0)
        block = jnp.where(col >= 2 * XE, 2, jnp.where(col >= XE, 1, 0))
        gap = col - block * XE - row
        band = jnp.zeros((CX, 3 * XE), F32)
        for i in range(TAPS):
            band = jnp.where(gap == i, kx[0, TAPS - 1 - i if reverse else i], band)
        high, low = two(band / total(kx, TAPS))
        band_x[...] = jnp.where(block == 1, low.astype(F32), high.astype(F32)).astype(BF16)
        gap = iota((CZ, CZ), 0) - iota((CZ, CZ), 1) + RZ
        band = jnp.zeros((CZ, CZ), F32)
        for i in range(ztaps):
            band = jnp.where(gap == i, kz[0, ztaps - 1 - i if reverse else i], band)
        high, low = two(band / total(kz, ztaps))
        band_z[...] = jnp.concatenate([high, low, high], axis=0)
        row = iota((ROWS, CZ), 0)
        table = jnp.zeros((ROWS, CZ), F32)
        for i in range(TAPS):
            table = jnp.where(row == i, ky[0, TAPS - 1 - i if reverse else i], table)
        taps[...] = table / total(ky, TAPS)


def smear_x(padded, count, band_x, lines, base):
    for y in range(0, count, 2):
        stack = []
        for k in range(2):
            high, low = two(padded[y + k])
            stack.append(jnp.concatenate([high, high, low], axis=0))
        both = mm(band_x[...], jnp.concatenate(stack, axis=1))
        lines[base + y] = both[:, :CZ]
        lines[base + y + 1] = both[:, CZ:]


def smear_yz(lines, base, taps, band_z, held):
    tap = [taps[i : i + 1, :] for i in range(TAPS)]

    def tile(t, carry):
        at = pl.ds(pl.multiple_of(t * 8, 8), 8)
        acc = [None] * HY
        for i in range(HY + 2 * R):
            value = lines[base + i, at, :]
            for y in range(HY):
                if 0 <= i - y < TAPS:
                    term = tap[i - y] * value
                    acc[y] = term if acc[y] is None else acc[y] + term
        for y in range(HY):
            held[y, at, :] = acc[y]
        return carry

    lax.fori_loop(0, CX // 8, tile, 0)
    high, low = two(held[...].reshape(HY * CX, CZ))
    result = mm(jnp.concatenate([high, high, low], axis=1), band_z[...])
    return [result[y * CX : (y + 1) * CX] for y in range(HY)]


def put_x(own, xa, xb, padded, count):
    odd_x, _ = sides()
    padded[:count, R : R + CX, :] = own[...]
    padded[:count, pl.ds(pl.multiple_of((1 - odd_x) * (CX + R), R), R), :] = xa[...]
    padded[:count, pl.ds(pl.multiple_of(odd_x * (CX + R), R), R), :] = xb[...]


def far_lines(own, x_halos, y_halos, band_x, padded, lines):
    _, odd_y = sides()
    put_x(own, *x_halos, padded, CY)
    smear_x(padded, CY, band_x, lines, R)
    far = (CY + R) * odd_y
    if y_halos:
        put_x(*y_halos, padded, R)
        smear_x(padded, R, band_x, lines, far)
    else:
        lines[pl.ds(far, R)] = jnp.zeros((R, CX, CZ), F32)


def near_lines(y_halos, band_x, padded, lines):
    _, odd_y = sides()
    put_x(*y_halos, padded, R)
    smear_x(padded, R, band_x, lines, (CY + R) * (1 - odd_y))


def blur_kernel(own, *refs):
    halos, (kx, ky, kz, out, *bands) = refs[:-13], refs[-13:]
    band_x, band_z, taps, padded, lines, held = bands[3:]
    make_bands(kx, ky, kz, *bands[3:6], *bands[:3])
    far_lines(own, halos[-2:], halos[3:-2], band_x, padded, lines)
    near_lines(halos[:3], band_x, padded, lines)
    for start in range(0, CY, HY):
        for y, value in enumerate(smear_yz(lines, start, taps, band_z, held)):
            out[start + y] = value


def put_quarters(values, mine, other, whole):
    core = lax.axis_index("view") % 2
    for y in range(HY):
        whole[pl.ds(y, CX, stride=HY), :] = values[y]
    rows = HX * HY
    other[...] = whole[pl.ds(pl.multiple_of((1 - core) * rows, rows), rows), :]
    mine[...] = whole[pl.ds(pl.multiple_of(core * rows, rows), rows), :]


def far_kernel(own, *refs):
    ins, (mine, other, lines, padded, held, whole) = refs[:-6], refs[-6:]
    halos, (band_x, band_z, taps) = ins[:-3], ins[-3:]
    _, odd_y = sides()
    far_lines(own, halos[-2:], halos[:-2], band_x, padded, lines)
    values = smear_yz(lines, HY * odd_y, taps, band_z, held)
    put_quarters(values, mine, other, whole)


def near_kernel(after, before, *refs):
    halos, (band_x, band_z, taps, mine, other, padded, held, whole, lines) = refs[:3], refs[3:]
    _, odd_y = sides()
    lines[R : R + CY] = before[R : R + CY]
    near_lines(halos, band_x, padded, lines)
    values = smear_yz(lines, HY * (1 - odd_y), taps, band_z, held)
    put_quarters(values, mine, other, whole)


def ratio_kernel(chunks, *refs):
    parts, blurred = refs[:chunks], refs[chunks]
    ratio, *edges = refs[chunks + 1 :]
    rows = chunks * GROUP
    metas = []
    for c in range(0, chunks, 2):
        odd = pltpu.roll(parts[c + 1][YP * GROUP :, :], GROUP, 1)
        metas.append(parts[c][YP * GROUP :, :] + odd)
    meta = jnp.concatenate(metas, axis=1)
    slot, count, weight = meta[0:1].astype(jnp.int32), meta[1:2].astype(jnp.int32), meta[2:3]
    key = (slot & (YP - 1)) * CX + (slot >> 2)
    chooser = (iota((SLOTS, rows), 0) == key).astype(F32).astype(BF16)
    keep = jnp.where(iota((CZ, rows), 0) < count, weight, 0.0).T

    def gathered(values):
        return sum(mm(chooser, part) for part in three(values))

    cover = gathered(keep)
    for j in range(0, YP, 2):
        values = jnp.concatenate(
            [
                jnp.concatenate([p[k * GROUP : (k + 1) * GROUP, :] for p in parts], axis=0)
                for k in (j, j + 1)
            ],
            axis=1,
        )
        data = gathered(values)
        for q in range(CY // YP):
            at = slice(q * CX, (q + 1) * CX)
            for k in range(2):
                y = YP * q + j + k
                base = blurred[y]
                ratio[y] = (data[at, k * CZ : (k + 1) * CZ] + PRIOR_WEIGHT * base) / (
                    (cover[at] + PRIOR_WEIGHT) * base
                )
    put_edges(ratio, edges)


def store_kernel(parts, *refs):
    ins, out, sems = refs[: len(parts)], refs[-2], refs[-1]
    core, (_, odd_y) = lax.axis_index("view") % 2, sides()
    copies = []
    for i, (part, near) in enumerate(parts):
        x = pl.multiple_of(HX * (core if part == 0 else 1 - core), HX)
        y = pl.multiple_of(HY * (1 - odd_y if near else odd_y), HY)
        to = out.at[pl.ds(x, HX), pl.ds(y, HY), :]
        copies.append(pltpu.make_async_copy(ins[i], to, sems.at[i]))
        copies[-1].start()
    for copy in copies:
        copy.wait()


def store(parts, values, before):
    def kernel(*refs):
        store_kernel(parts, *refs)

    values = [value.reshape(HX, HY, CZ) for value in values]
    specs, aliases = [VM] * len(values), {}
    if before is not None:
        values.append(before)
        specs.append(ANY)
        aliases = {len(parts): 0}
    sems = [pltpu.SemaphoreType.DMA((len(parts),))]
    return call(kernel, [(CX, CY, CZ)], sems, specs, [ANY], aliases)(*values)[0]


def swap(x, axis, mask):
    return lax.ppermute(x, axis, [(i, i ^ mask) for i in range(lax.axis_size(axis))])


def pairs(axis):
    count = lax.axis_size(axis)
    first = [(i, i ^ 1) for i in range(count) if i ^ 1 < count]
    second = [(i, ((i + 1) ^ 1) - 1) for i in range(count)]
    second = [(i, k) for i, k in second if 0 <= k < count]
    return [first] + ([second] if second else [])


def halo_pairs():
    x_pairs, y_pairs, wide = pairs("bx"), pairs("by"), lax.axis_size("by")
    x_pairs = x_pairs + [[]] * (2 - len(x_pairs))
    out = []
    for ys in y_pairs:
        out.append(("by", ys))
        for xs in x_pairs:
            moves = [(a * wide + c, b * wide + d) for a, b in xs for c, d in ys]
            out.append((("bx", "by"), moves))
    return out + [("bx", xs) for xs in x_pairs]


def halo(edges):
    got = []
    for edge, (axis, moves) in zip(edges, halo_pairs()):
        got.append(lax.ppermute(edge, axis, moves) if moves else jnp.zeros_like(edge))
    return got


def generic_exchange(bricks, observed, target, slot, count, weight):
    capacity = max(4, 2 * PIECES // bricks)
    member = (target[:, None] == jnp.arange(bricks)[None, :]).astype(jnp.int32)
    slot_rank = jnp.sum((jnp.cumsum(member, axis=0) - 1) * member, axis=1)
    place = target * capacity + slot_rank
    keep = jnp.where(jnp.arange(CZ)[None, :] < count[:, None], weight[:, None], 0.0)
    weighted = (observed.reshape(-1, YP, CZ) * keep[:, None, :]).reshape(-1, PV)
    facts = jnp.stack([slot.astype(F32), count.astype(F32), weight], axis=1)
    rows = jnp.zeros((bricks * capacity, PV), F32).at[place].set(weighted)
    facts = jnp.zeros((bricks * capacity, 3), F32).at[place].set(facts)

    def exchange(x):
        x = x.reshape(bricks, capacity, -1)
        return lax.all_to_all(x, ("bx", "by"), split_axis=0, concat_axis=0, tiled=True)

    chunks = bricks * capacity // GROUP
    rows = exchange(rows).reshape(chunks, GROUP, YP, CZ).transpose(0, 2, 1, 3)
    facts = exchange(facts).reshape(chunks, GROUP, 3).transpose(0, 2, 1)
    facts = jnp.pad(facts, ((0, 0), (0, 5), (0, CZ - GROUP)))
    both = jnp.concatenate([rows.reshape(chunks, YP * GROUP, CZ), facts], axis=1)
    return [both[c] for c in range(chunks)]


def local(
    estimate,
    observed,
    destination,
    slot_index,
    valid_count,
    blend_weight,
    kernel_x,
    kernel_y,
    kernel_z,
):
    count_bx, count_by = lax.axis_size("bx"), lax.axis_size("by")
    bricks = count_bx * count_by
    phases = len(pairs("by"))
    flat = estimate.reshape(CX * CY, CZ)
    edge_shapes = [(R, CX, CZ), (R, R, CZ), (R, R, CZ)] * phases + [(CY, R, CZ)] * 2
    brick, quarter, lines = (CY, CX, CZ), (HX * HY, CZ), (CY + 2 * R, CX, CZ)
    padded, held = pltpu.VMEM((CY, XE, CZ), F32), pltpu.VMEM((HY, CX, CZ), F32)
    whole = pltpu.VMEM((CX * HY, CZ), F32)

    if bricks * GROUP == 2 * PIECES:
        room = [pltpu.VMEM((PIECES, PV), F32)]
        room += [pltpu.VMEM((1, PIECES), jnp.int32)] * 3 + [pltpu.VMEM((1, PIECES), F32)]
        room.append(pltpu.SemaphoreType.DMA((5,)))
        shapes = [(CHUNK, CZ)] * bricks + [(8, CZ)]
        *packed, token = call(pack_kernel, shapes, room, [HB] * 5, limit=PACK_LIMIT)(
            *[
                pltpu.with_memory_space_constraint(x, pltpu.HBM)
                for x in (
                    observed[0],
                    destination.reshape(1, PIECES),
                    slot_index,
                    valid_count,
                    blend_weight,
                )
            ]
        )
        chunks = [packed[0]]
        for s in sorted(range(1, bricks), reverse=True):
            pair = [(d, d ^ s) for d in range(bricks)]
            chunks.append(lax.ppermute(packed[s], ("bx", "by"), pair))
    else:
        token = jnp.zeros((8, CZ), F32)
        chunks = generic_exchange(
            bricks,
            observed[0],
            destination[0, :, 0],
            slot_index[0],
            valid_count[0],
            blend_weight[0],
        )

    turned, *edges = call(turn_kernel, [brick] + edge_shapes, in_specs=[VM, ANY])(flat, token)
    around = halo(edges)
    bands = [((CX, 3 * XE), BF16), ((3 * CZ, CZ), BF16), ((ROWS, CZ), F32)]
    work = [pltpu.VMEM(*band) for band in bands] + [padded, pltpu.VMEM(lines, F32), held]
    shapes = [brick] + [jax.ShapeDtypeStruct(*band) for band in bands]
    specs = [VM] * (len(around) + 1) + [SM] * 3
    blurred, *bands = call(blur_kernel, shapes, work, specs, limit=BLUR_LIMIT)(
        turned, *around, kernel_x, kernel_y, kernel_z
    )

    def ratios(*refs):
        ratio_kernel(len(chunks), *refs)

    ratio, *edges = call(ratios, [brick] + edge_shapes, in_specs=[VM] * (len(chunks) + 1))(
        *chunks, blurred
    )
    around = halo(edges)
    near_halos, far_halos = around[:3], around[3:]
    mine, other, before = call(
        far_kernel, [quarter, quarter, lines], [padded, held, whole], [VM] * (len(far_halos) + 4)
    )(ratio, *far_halos, *bands)
    core, odd_y = lax.axis_index("view") % 2, lax.axis_index("by") % 2

    def paired(mine, other):
        return mine * swap(other, "view", 1)

    def product(mine, start, estimate):
        across = swap(mine, "view", 2)
        own = lax.dynamic_slice(estimate, (core * HX, start * HY, 0), (HX, HY, CZ))
        mine = mine * across * own.reshape(HX * HY, CZ)
        return mine, swap(mine, "view", 1)

    mine = paired(mine, other)
    work = [padded, held, whole, pltpu.VMEM(lines, F32)]
    near = call(near_kernel, [quarter, quarter], work, [ANY] + [VM] * 7)(
        mine, before, *near_halos, *bands
    )
    far_mine, far_other = product(mine, odd_y, estimate)
    updated = store([(0, False), (1, False)], [far_mine, far_other], None)
    estimate, far_mine = lax.optimization_barrier((estimate, far_mine))
    near_mine, near_other = product(paired(*near), 1 - odd_y, estimate)
    updated = store([(0, True)], [near_mine], updated)
    return store([(1, True)], [near_other], updated)


def solution(mesh):
    placed = (
        P("bx", "by", None),
        P("view", ("bx", "by"), None),
        P("view", ("bx", "by"), None),
        P("view", ("bx", "by")),
        P("view", ("bx", "by")),
        P("view", ("bx", "by")),
        P("view", None),
        P("view", None),
        P("view", None),
    )

    return jax.shard_map(
        local, mesh=mesh, in_specs=placed, out_specs=P("bx", "by", None), check_vma=False
    )
```

```python
import jax
import jax.numpy as jnp
from jax import lax
from jax.experimental import pallas as pl
from jax.experimental.pallas import tpu as pltpu
from jax.sharding import PartitionSpec as P


R = 8
RZ = 16
YP = 4
PV = 512
SLOTS = 256
PIECES = 256
CX = 64
CY = 16
CZ = 128
PRIOR_WEIGHT = 0.5
F32 = jnp.float32
BF16 = jnp.bfloat16
VM = pl.BlockSpec(memory_space=pltpu.VMEM)
SM = pl.BlockSpec(memory_space=pltpu.SMEM)
ANY = pl.BlockSpec(memory_space=pl.ANY)
HB = pl.BlockSpec(memory_space=pltpu.HBM)
HX = CX // 2
HY = CY // 2
XE = CX + 2 * R
TAPS = 2 * R + 1
ROWS = 24
PACK_LIMIT = 32 << 20
BLUR_LIMIT = 32 << 20
GROUP = 64
CHUNK = YP * GROUP + 8


def call(
    kernel,
    outs,
    scratch=(),
    in_specs=None,
    out_specs=None,
    aliases=None,
    limit=32 << 20,
    flops=1 << 22,
    moved=1 << 20,
):
    shapes = [o if hasattr(o, "dtype") else jax.ShapeDtypeStruct(o, F32) for o in outs]
    return pl.pallas_call(
        kernel,
        out_shape=shapes,
        in_specs=in_specs,
        out_specs=out_specs or [VM] * len(outs),
        scratch_shapes=list(scratch),
        input_output_aliases=aliases or {},
        compiler_params=pltpu.CompilerParams(vmem_limit_bytes=limit),
        cost_estimate=pl.CostEstimate(flops=flops, bytes_accessed=moved, transcendentals=0),
    )


def three(x):
    high = x.astype(BF16)
    rest = x - high.astype(F32)
    mid = rest.astype(BF16)
    return high, mid, (rest - mid.astype(F32)).astype(BF16)


def two(x):
    high = x.astype(BF16)
    return high, (x - high.astype(F32)).astype(BF16)


def iota(shape, dim):
    return lax.broadcasted_iota(jnp.int32, shape, dim)


def mm(a, b):
    return jnp.dot(a, b, preferred_element_type=F32)


def pack_kernel(*refs):
    sources, outs, token, held, sems = refs[:5], refs[5:-7], refs[-7], refs[-6:-1], refs[-1]
    bricks = len(outs)
    token[...] = jnp.zeros((8, CZ), F32)
    copies = [
        pltpu.make_async_copy(source, to, sems.at[i])
        for i, (source, to) in enumerate(zip(sources, held))
    ]
    for copy in copies:
        copy.start()
    observed, target, slot, count, weight = held
    for copy in copies[1:]:
        copy.wait()
    me = lax.axis_index("bx") * lax.axis_size("by") + lax.axis_index("by")
    goal = target[...] ^ me
    member = (iota((bricks, PIECES), 0) == goal).astype(F32)
    upto = (iota((PIECES, PIECES), 0) <= iota((PIECES, PIECES), 1)).astype(F32)
    ranks = mm(member.astype(BF16), upto.astype(BF16))
    rank = jnp.sum(member * ranks, axis=0, keepdims=True).astype(jnp.int32) - 1
    place = goal * GROUP + rank
    rows = bricks * GROUP
    pick = (iota((rows, PIECES), 0) == place).astype(F32).astype(BF16)
    keep = jnp.where(iota((CZ, PIECES), 0) < count[...], weight[...], 0.0).T
    copies[0].wait()
    weighted = observed[...] * jnp.concatenate([keep] * YP, axis=1)
    packed = sum(mm(pick, part) for part in three(weighted))
    parts = [p.astype(F32) for p in three(weight[...])]
    table = jnp.concatenate(
        [slot[...].astype(F32), count[...].astype(F32)] + parts + [jnp.zeros((3, PIECES), F32)],
        axis=0,
    )
    meta = lax.dot_general(
        table.astype(BF16), pick, (((1,), (1,)), ((), ())), preferred_element_type=F32
    )
    wide = jnp.concatenate(
        [meta[0:2], meta[2:3] + meta[3:4] + meta[4:5], jnp.zeros((5, rows), F32)], axis=0
    )
    lane = iota((8, CZ), 1)
    for s in range(bricks):
        for j in range(YP):
            outs[s][j * GROUP : (j + 1) * GROUP, :] = packed[
                s * GROUP : (s + 1) * GROUP, j * CZ : (j + 1) * CZ
            ]
        pair = wide[:, (s // 2) * CZ : (s // 2 + 1) * CZ]
        if s % 2:
            pair = pltpu.roll(pair, GROUP, 1)
        outs[s][YP * GROUP :, :] = jnp.where(lane < GROUP, pair, 0.0)


def sides():
    odd_x = lax.axis_index("bx") % 2
    odd_y = lax.axis_index("by") % 2
    return odd_x, odd_y


def put_edges(volume, outs):
    odd_x, odd_y = sides()
    for phase, out in enumerate(outs[:-2]):
        out[...] = volume[pl.ds((odd_y if phase else 1 - odd_y) * (CY - R), R)]
    for phase, out in enumerate(outs[-2:]):
        at = (odd_x if phase else 1 - odd_x) * (CX - R)
        out[...] = volume[:, pl.ds(pl.multiple_of(at, R), R), :]


def corner_kernel(xa, xb, *outs):
    _, odd_y = sides()
    for phase, out in enumerate(outs):
        rows = pl.ds((odd_y if phase else 1 - odd_y) * (CY - R), R)
        out[0] = xa[rows]
        out[1] = xb[rows]


def turn_kernel(estimate, after, turned, *edges):
    for y in range(CY):
        turned[y] = estimate[pl.ds(y, CX, stride=CY), :]
    put_edges(turned, edges)


def total(kernel, taps):
    acc = kernel[0, 0]
    for i in range(1, taps):
        acc = acc + kernel[0, i]
    return acc


def make_bands(kx, ky, kz, *outs):
    ztaps = 2 * RZ + 1
    for reverse in range(2):
        band_x, band_z, taps = outs[3 * reverse : 3 * reverse + 3]
        col, row = iota((CX, 3 * XE), 1), iota((CX, 3 * XE), 0)
        block = jnp.where(col >= 2 * XE, 2, jnp.where(col >= XE, 1, 0))
        gap = col - block * XE - row
        band = jnp.zeros((CX, 3 * XE), F32)
        for i in range(TAPS):
            band = jnp.where(gap == i, kx[0, TAPS - 1 - i if reverse else i], band)
        high, low = two(band / total(kx, TAPS))
        band_x[...] = jnp.where(block == 1, low.astype(F32), high.astype(F32)).astype(BF16)
        gap = iota((CZ, CZ), 0) - iota((CZ, CZ), 1) + RZ
        band = jnp.zeros((CZ, CZ), F32)
        for i in range(ztaps):
            band = jnp.where(gap == i, kz[0, ztaps - 1 - i if reverse else i], band)
        high, low = two(band / total(kz, ztaps))
        band_z[...] = jnp.concatenate([high, low, high], axis=0)
        row = iota((ROWS, CZ), 0)
        table = jnp.zeros((ROWS, CZ), F32)
        for i in range(TAPS):
            table = jnp.where(row == i, ky[0, TAPS - 1 - i if reverse else i], table)
        taps[...] = table / total(ky, TAPS)


def smear_x(padded, count, band_x, lines, base):
    for y in range(0, count, 2):
        stack = []
        for k in range(2):
            high, low = two(padded[y + k])
            stack.append(jnp.concatenate([high, high, low], axis=0))
        both = mm(band_x[...], jnp.concatenate(stack, axis=1))
        lines[base + y] = both[:, :CZ]
        lines[base + y + 1] = both[:, CZ:]


def smear_yz(lines, base, taps, band_z, held):
    tap = [taps[i : i + 1, :] for i in range(TAPS)]

    def tile(t, carry):
        at = pl.ds(pl.multiple_of(t * 8, 8), 8)
        acc = [None] * HY
        for i in range(HY + 2 * R):
            value = lines[base + i, at, :]
            for y in range(HY):
                if 0 <= i - y < TAPS:
                    term = tap[i - y] * value
                    acc[y] = term if acc[y] is None else acc[y] + term
        for y in range(HY):
            held[y, at, :] = acc[y]
        return carry

    lax.fori_loop(0, CX // 8, tile, 0)
    high, low = two(held[...].reshape(HY * CX, CZ))
    result = mm(jnp.concatenate([high, high, low], axis=1), band_z[...])
    return [result[y * CX : (y + 1) * CX] for y in range(HY)]


def put_x(own, xa, xb, padded, count):
    odd_x, _ = sides()
    padded[:count, R : R + CX, :] = own[...]
    padded[:count, pl.ds(pl.multiple_of((1 - odd_x) * (CX + R), R), R), :] = xa[...]
    padded[:count, pl.ds(pl.multiple_of(odd_x * (CX + R), R), R), :] = xb[...]


def far_lines(own, x_halos, y_halo, band_x, padded, lines):
    _, odd_y = sides()
    put_x(own, *x_halos, padded, CY)
    smear_x(padded, CY, band_x, lines, R)
    far = (CY + R) * odd_y
    if y_halo:
        put_x(y_halo[0], y_halo[1].at[0], y_halo[1].at[1], padded, R)
        smear_x(padded, R, band_x, lines, far)
    else:
        lines[pl.ds(far, R)] = jnp.zeros((R, CX, CZ), F32)


def near_lines(y_halo, band_x, padded, lines):
    _, odd_y = sides()
    put_x(y_halo[0], y_halo[1].at[0], y_halo[1].at[1], padded, R)
    smear_x(padded, R, band_x, lines, (CY + R) * (1 - odd_y))


def blur_kernel(own, *refs):
    halos, (kx, ky, kz, out, *bands) = refs[:-13], refs[-13:]
    band_x, band_z, taps, padded, lines, held = bands[3:]
    make_bands(kx, ky, kz, *bands[3:6], *bands[:3])
    far_lines(own, halos[-2:], halos[2:-2], band_x, padded, lines)
    near_lines(halos[:2], band_x, padded, lines)
    for start in range(0, CY, HY):
        for y, value in enumerate(smear_yz(lines, start, taps, band_z, held)):
            out[start + y] = value


def put_quarters(values, mine, other, whole):
    core = lax.axis_index("view") % 2
    for y in range(HY):
        whole[pl.ds(y, CX, stride=HY), :] = values[y]
    rows = HX * HY
    other[...] = whole[pl.ds(pl.multiple_of((1 - core) * rows, rows), rows), :]
    mine[...] = whole[pl.ds(pl.multiple_of(core * rows, rows), rows), :]


def far_kernel(own, *refs):
    ins, (mine, other, lines, padded, held, whole) = refs[:-6], refs[-6:]
    halos, (band_x, band_z, taps) = ins[:-3], ins[-3:]
    _, odd_y = sides()
    far_lines(own, halos[-2:], halos[:-2], band_x, padded, lines)
    values = smear_yz(lines, HY * odd_y, taps, band_z, held)
    put_quarters(values, mine, other, whole)


def near_kernel(after, before, *refs):
    halos, (band_x, band_z, taps, mine, other, padded, held, whole, lines) = refs[:2], refs[2:]
    _, odd_y = sides()
    lines[R : R + CY] = before[R : R + CY]
    near_lines(halos, band_x, padded, lines)
    values = smear_yz(lines, HY * (1 - odd_y), taps, band_z, held)
    put_quarters(values, mine, other, whole)


def ratio_kernel(chunks, *refs):
    parts, blurred = refs[:chunks], refs[chunks]
    ratio, *edges = refs[chunks + 1 :]
    rows = chunks * GROUP
    metas = []
    for c in range(0, chunks, 2):
        odd = pltpu.roll(parts[c + 1][YP * GROUP :, :], GROUP, 1)
        metas.append(parts[c][YP * GROUP :, :] + odd)
    meta = jnp.concatenate(metas, axis=1)
    slot, count, weight = meta[0:1].astype(jnp.int32), meta[1:2].astype(jnp.int32), meta[2:3]
    key = (slot & (YP - 1)) * CX + (slot >> 2)
    chooser = (iota((SLOTS, rows), 0) == key).astype(F32).astype(BF16)
    keep = jnp.where(iota((CZ, rows), 0) < count, weight, 0.0).T

    def gathered(values):
        return sum(mm(chooser, part) for part in three(values))

    cover = gathered(keep)
    for j in range(0, YP, 2):
        values = jnp.concatenate(
            [
                jnp.concatenate([p[k * GROUP : (k + 1) * GROUP, :] for p in parts], axis=0)
                for k in (j, j + 1)
            ],
            axis=1,
        )
        data = gathered(values)
        for q in range(CY // YP):
            at = slice(q * CX, (q + 1) * CX)
            for k in range(2):
                y = YP * q + j + k
                base = blurred[y]
                ratio[y] = (data[at, k * CZ : (k + 1) * CZ] + PRIOR_WEIGHT * base) / (
                    (cover[at] + PRIOR_WEIGHT) * base
                )
    put_edges(ratio, edges)


def store_kernel(parts, *refs):
    ins, out, sems = refs[: len(parts)], refs[-2], refs[-1]
    core, (_, odd_y) = lax.axis_index("view") % 2, sides()
    copies = []
    for i, (part, near) in enumerate(parts):
        x = pl.multiple_of(HX * (core if part == 0 else 1 - core), HX)
        y = pl.multiple_of(HY * (1 - odd_y if near else odd_y), HY)
        to = out.at[pl.ds(x, HX), pl.ds(y, HY), :]
        copies.append(pltpu.make_async_copy(ins[i], to, sems.at[i]))
        copies[-1].start()
    for copy in copies:
        copy.wait()


def store(parts, values, before):
    def kernel(*refs):
        store_kernel(parts, *refs)

    values = [value.reshape(HX, HY, CZ) for value in values]
    specs, aliases = [VM] * len(values), {}
    if before is not None:
        values.append(before)
        specs.append(ANY)
        aliases = {len(parts): 0}
    sems = [pltpu.SemaphoreType.DMA((len(parts),))]
    return call(kernel, [(CX, CY, CZ)], sems, specs, [ANY], aliases)(*values)[0]


def swap(x, axis, mask):
    return lax.ppermute(x, axis, [(i, i ^ mask) for i in range(lax.axis_size(axis))])


def pairs(axis):
    count = lax.axis_size(axis)
    first = [(i, i ^ 1) for i in range(count) if i ^ 1 < count]
    second = [(i, ((i + 1) ^ 1) - 1) for i in range(count)]
    second = [(i, k) for i, k in second if 0 <= k < count]
    return [first] + ([second] if second else [])


def halo(edges):
    x_pairs, y_pairs = pairs("bx"), pairs("by")
    x_pairs = x_pairs + [[]] * (2 - len(x_pairs))

    def move(value, axis, moves):
        return lax.ppermute(value, axis, moves) if moves else jnp.zeros_like(value)

    got_y = [move(e, "by", p) for e, p in zip(edges, y_pairs)]
    got_x = [move(e, "bx", p) for e, p in zip(edges[-2:], x_pairs)]
    cut = call(corner_kernel, [(2, R, R, CZ)] * len(y_pairs), in_specs=[VM] * 2)(*got_x)
    got_c = [move(e, "by", p) for e, p in zip(cut, y_pairs)]
    return [value for both in zip(got_y, got_c) for value in both] + got_x


def generic_exchange(bricks, observed, target, slot, count, weight):
    capacity = max(4, 2 * PIECES // bricks)
    member = (target[:, None] == jnp.arange(bricks)[None, :]).astype(jnp.int32)
    slot_rank = jnp.sum((jnp.cumsum(member, axis=0) - 1) * member, axis=1)
    place = target * capacity + slot_rank
    keep = jnp.where(jnp.arange(CZ)[None, :] < count[:, None], weight[:, None], 0.0)
    weighted = (observed.reshape(-1, YP, CZ) * keep[:, None, :]).reshape(-1, PV)
    facts = jnp.stack([slot.astype(F32), count.astype(F32), weight], axis=1)
    rows = jnp.zeros((bricks * capacity, PV), F32).at[place].set(weighted)
    facts = jnp.zeros((bricks * capacity, 3), F32).at[place].set(facts)

    def exchange(x):
        x = x.reshape(bricks, capacity, -1)
        return lax.all_to_all(x, ("bx", "by"), split_axis=0, concat_axis=0, tiled=True)

    chunks = bricks * capacity // GROUP
    rows = exchange(rows).reshape(chunks, GROUP, YP, CZ).transpose(0, 2, 1, 3)
    facts = exchange(facts).reshape(chunks, GROUP, 3).transpose(0, 2, 1)
    facts = jnp.pad(facts, ((0, 0), (0, 5), (0, CZ - GROUP)))
    both = jnp.concatenate([rows.reshape(chunks, YP * GROUP, CZ), facts], axis=1)
    return [both[c] for c in range(chunks)]


def local(
    estimate,
    observed,
    destination,
    slot_index,
    valid_count,
    blend_weight,
    kernel_x,
    kernel_y,
    kernel_z,
):
    count_bx, count_by = lax.axis_size("bx"), lax.axis_size("by")
    bricks = count_bx * count_by
    phases = len(pairs("by"))
    flat = estimate.reshape(CX * CY, CZ)
    edge_shapes = [(R, CX, CZ)] * phases + [(CY, R, CZ)] * 2
    brick, quarter, lines = (CY, CX, CZ), (HX * HY, CZ), (CY + 2 * R, CX, CZ)
    padded, held = pltpu.VMEM((CY, XE, CZ), F32), pltpu.VMEM((HY, CX, CZ), F32)
    whole = pltpu.VMEM((CX * HY, CZ), F32)

    if bricks * GROUP == 2 * PIECES:
        room = [pltpu.VMEM((PIECES, PV), F32)]
        room += [pltpu.VMEM((1, PIECES), jnp.int32)] * 3 + [pltpu.VMEM((1, PIECES), F32)]
        room.append(pltpu.SemaphoreType.DMA((5,)))
        shapes = [(CHUNK, CZ)] * bricks + [(8, CZ)]
        *packed, token = call(pack_kernel, shapes, room, [HB] * 5, limit=PACK_LIMIT)(
            *[
                pltpu.with_memory_space_constraint(x, pltpu.HBM)
                for x in (
                    observed[0],
                    destination.reshape(1, PIECES),
                    slot_index,
                    valid_count,
                    blend_weight,
                )
            ]
        )
        chunks = [packed[0]]
        for s in sorted(range(1, bricks), reverse=True):
            pair = [(d, d ^ s) for d in range(bricks)]
            chunks.append(lax.ppermute(packed[s], ("bx", "by"), pair))
    else:
        token = jnp.zeros((8, CZ), F32)
        chunks = generic_exchange(
            bricks,
            observed[0],
            destination[0, :, 0],
            slot_index[0],
            valid_count[0],
            blend_weight[0],
        )

    turned, *edges = call(turn_kernel, [brick] + edge_shapes, in_specs=[VM, ANY])(flat, token)
    around = halo(edges)
    bands = [((CX, 3 * XE), BF16), ((3 * CZ, CZ), BF16), ((ROWS, CZ), F32)]
    work = [pltpu.VMEM(*band) for band in bands] + [padded, pltpu.VMEM(lines, F32), held]
    shapes = [brick] + [jax.ShapeDtypeStruct(*band) for band in bands]
    specs = [VM] * (len(around) + 1) + [SM] * 3
    blurred, *bands = call(blur_kernel, shapes, work, specs, limit=BLUR_LIMIT)(
        turned, *around, kernel_x, kernel_y, kernel_z
    )

    def ratios(*refs):
        ratio_kernel(len(chunks), *refs)

    ratio, *edges = call(ratios, [brick] + edge_shapes, in_specs=[VM] * (len(chunks) + 1))(
        *chunks, blurred
    )
    around = halo(edges)
    near_halos, far_halos = around[:2], around[2:]
    mine, other, before = call(
        far_kernel,
        [quarter, quarter, lines],
        [padded, held, whole],
        [VM] * (len(far_halos) + 4),
    )(ratio, *far_halos, *bands)
    core, odd_y = lax.axis_index("view") % 2, lax.axis_index("by") % 2

    def paired(mine, other):
        return mine * swap(other, "view", 1)

    def product(mine, start, estimate):
        across = swap(mine, "view", 2)
        own = lax.dynamic_slice(estimate, (core * HX, start * HY, 0), (HX, HY, CZ))
        mine = mine * across * own.reshape(HX * HY, CZ)
        return mine, swap(mine, "view", 1)

    mine = paired(mine, other)
    work = [padded, held, whole, pltpu.VMEM(lines, F32)]
    near = call(near_kernel, [quarter, quarter], work, [ANY] + [VM] * 6)(
        mine, before, *near_halos, *bands
    )
    far_mine, far_other = product(mine, odd_y, estimate)
    updated = store([(0, False), (1, False)], [far_mine, far_other], None)
    estimate, far_mine = lax.optimization_barrier((estimate, far_mine))
    near_mine, near_other = product(paired(*near), 1 - odd_y, estimate)
    updated = store([(0, True)], [near_mine], updated)
    return store([(1, True)], [near_other], updated)


def solution(mesh):
    placed = (
        P("bx", "by", None),
        P("view", ("bx", "by"), None),
        P("view", ("bx", "by"), None),
        P("view", ("bx", "by")),
        P("view", ("bx", "by")),
        P("view", ("bx", "by")),
        P("view", None),
        P("view", None),
        P("view", None),
    )

    return jax.shard_map(
        local, mesh=mesh, in_specs=placed, out_specs=P("bx", "by", None), check_vma=False
    )
```

```python
import jax
import jax.numpy as jnp
from jax import lax
from jax.experimental import pallas as pl
from jax.experimental.pallas import tpu as pltpu
from jax.sharding import PartitionSpec as P


R = 8
RZ = 16
YP = 4
PV = 512
SLOTS = 256
PIECES = 256
CX = 64
CY = 16
CZ = 128
PRIOR_WEIGHT = 0.5
F32 = jnp.float32
BF16 = jnp.bfloat16
VM = pl.BlockSpec(memory_space=pltpu.VMEM)
SM = pl.BlockSpec(memory_space=pltpu.SMEM)
ANY = pl.BlockSpec(memory_space=pl.ANY)
HB = pl.BlockSpec(memory_space=pltpu.HBM)
HX = CX // 2
HY = CY // 2
XE = CX + 2 * R
TAPS = 2 * R + 1
ROWS = 24
PACK_LIMIT = 32 << 20
GROUP = 64
CHUNK = YP * GROUP + 8


def call(
    kernel,
    outs,
    scratch=(),
    in_specs=None,
    out_specs=None,
    aliases=None,
    limit=32 << 20,
    flops=1 << 22,
    moved=1 << 20,
):
    shapes = [o if hasattr(o, "dtype") else jax.ShapeDtypeStruct(o, F32) for o in outs]
    return pl.pallas_call(
        kernel,
        out_shape=shapes,
        in_specs=in_specs,
        out_specs=out_specs or [VM] * len(outs),
        scratch_shapes=list(scratch),
        input_output_aliases=aliases or {},
        compiler_params=pltpu.CompilerParams(vmem_limit_bytes=limit),
        cost_estimate=pl.CostEstimate(flops=flops, bytes_accessed=moved, transcendentals=0),
    )


def three(x):
    high = x.astype(BF16)
    rest = x - high.astype(F32)
    mid = rest.astype(BF16)
    return high, mid, (rest - mid.astype(F32)).astype(BF16)


def two(x):
    high = x.astype(BF16)
    return high, (x - high.astype(F32)).astype(BF16)


def iota(shape, dim):
    return lax.broadcasted_iota(jnp.int32, shape, dim)


def mm(a, b):
    return jnp.dot(a, b, preferred_element_type=F32)


def pack_kernel(*refs):
    sources, outs, token, held, sems = refs[:5], refs[5:-7], refs[-7], refs[-6:-1], refs[-1]
    bricks = len(outs)
    token[...] = jnp.zeros((8, CZ), F32)
    copies = [
        pltpu.make_async_copy(source, to, sems.at[i])
        for i, (source, to) in enumerate(zip(sources, held))
    ]
    for copy in copies:
        copy.start()
    observed, target, slot, count, weight = held
    for copy in copies[1:]:
        copy.wait()
    me = lax.axis_index("bx") * lax.axis_size("by") + lax.axis_index("by")
    goal = target[...] ^ me
    member = (iota((bricks, PIECES), 0) == goal).astype(F32)
    upto = (iota((PIECES, PIECES), 0) <= iota((PIECES, PIECES), 1)).astype(F32)
    ranks = mm(member.astype(BF16), upto.astype(BF16))
    rank = jnp.sum(member * ranks, axis=0, keepdims=True).astype(jnp.int32) - 1
    place = goal * GROUP + rank
    rows = bricks * GROUP
    pick = (iota((rows, PIECES), 0) == place).astype(F32).astype(BF16)
    keep = jnp.where(iota((CZ, PIECES), 0) < count[...], weight[...], 0.0).T
    copies[0].wait()
    weighted = observed[...] * jnp.concatenate([keep] * YP, axis=1)
    packed = sum(mm(pick, part) for part in three(weighted))
    parts = [p.astype(F32) for p in three(weight[...])]
    table = jnp.concatenate(
        [slot[...].astype(F32), count[...].astype(F32)] + parts + [jnp.zeros((3, PIECES), F32)],
        axis=0,
    )
    meta = lax.dot_general(
        table.astype(BF16), pick, (((1,), (1,)), ((), ())), preferred_element_type=F32
    )
    wide = jnp.concatenate(
        [meta[0:2], meta[2:3] + meta[3:4] + meta[4:5], jnp.zeros((5, rows), F32)], axis=0
    )
    lane = iota((8, CZ), 1)
    for s in range(bricks):
        for j in range(YP):
            outs[s][j * GROUP : (j + 1) * GROUP, :] = packed[
                s * GROUP : (s + 1) * GROUP, j * CZ : (j + 1) * CZ
            ]
        pair = wide[:, (s // 2) * CZ : (s // 2 + 1) * CZ]
        if s % 2:
            pair = pltpu.roll(pair, GROUP, 1)
        outs[s][YP * GROUP :, :] = jnp.where(lane < GROUP, pair, 0.0)


def sides():
    odd_x = lax.axis_index("bx") % 2
    odd_y = lax.axis_index("by") % 2
    return odd_x, odd_y


def put_edges(volume, outs):
    odd_x, odd_y = sides()
    for phase, out in enumerate(outs[:-2]):
        out[...] = volume[pl.ds((odd_y if phase else 1 - odd_y) * (CY - R), R)]
    for phase, out in enumerate(outs[-2:]):
        at = (odd_x if phase else 1 - odd_x) * (CX - R)
        out[...] = volume[:, pl.ds(pl.multiple_of(at, R), R), :]


def corner_kernel(xa, xb, *outs):
    _, odd_y = sides()
    for phase, out in enumerate(outs):
        rows = pl.ds((odd_y if phase else 1 - odd_y) * (CY - R), R)
        out[0] = xa[rows]
        out[1] = xb[rows]


def turn_kernel(estimate, after, turned, edge_x, *edges_y):
    for y in range(CY):
        turned[y] = estimate[pl.ds(y, CX, stride=CY), :]
    odd_x, odd_y = sides()
    core = lax.axis_index("view") % 2
    at = jnp.where(core == 0, 1 - odd_x, odd_x) * (CX - R)
    edge_x[...] = turned[:, pl.ds(pl.multiple_of(at, R), R), :]
    for phase, out in enumerate(edges_y):
        at = (odd_y if phase else 1 - odd_y) * (CY - R) + core * (R // 2)
        out[...] = turned[pl.ds(at, R // 2)]


def cut_kernel(got, *outs):
    _, odd_y = sides()
    for phase, out in enumerate(outs):
        out[...] = got[pl.ds((odd_y if phase else 1 - odd_y) * (CY - R), R)]


def total(kernel, taps):
    acc = kernel[0, 0]
    for i in range(1, taps):
        acc = acc + kernel[0, i]
    return acc


def band_kernel(kx, ky, kz, *outs):
    ztaps = 2 * RZ + 1
    for reverse in range(2):
        band_x, band_z, taps = outs[3 * reverse : 3 * reverse + 3]
        col, row = iota((CX, 3 * XE), 1), iota((CX, 3 * XE), 0)
        block = jnp.where(col >= 2 * XE, 2, jnp.where(col >= XE, 1, 0))
        gap = col - block * XE - row
        band = jnp.zeros((CX, 3 * XE), F32)
        for i in range(TAPS):
            band = jnp.where(gap == i, kx[0, TAPS - 1 - i if reverse else i], band)
        high, low = two(band / total(kx, TAPS))
        band_x[...] = jnp.where(block == 1, low.astype(F32), high.astype(F32)).astype(BF16)
        gap = iota((CZ, CZ), 0) - iota((CZ, CZ), 1) + RZ
        band = jnp.zeros((CZ, CZ), F32)
        for i in range(ztaps):
            band = jnp.where(gap == i, kz[0, ztaps - 1 - i if reverse else i], band)
        high, low = two(band / total(kz, ztaps))
        band_z[...] = jnp.concatenate([high, low, high], axis=0)
        row = iota((ROWS, CZ), 0)
        table = jnp.zeros((ROWS, CZ), F32)
        for i in range(TAPS):
            table = jnp.where(row == i, ky[0, TAPS - 1 - i if reverse else i], table)
        taps[...] = table / total(ky, TAPS)


def smear_x(padded, count, band_x, lines, base):
    for y in range(0, count, 2):
        stack = []
        for k in range(2):
            high, low = two(padded[y + k])
            stack.append(jnp.concatenate([high, high, low], axis=0))
        both = mm(band_x[...], jnp.concatenate(stack, axis=1))
        lines[base + y] = both[:, :CZ]
        lines[base + y + 1] = both[:, CZ:]


def smear_yz(lines, base, taps, band_z, held):
    tap = [taps[i : i + 1, :] for i in range(TAPS)]

    def tile(t, carry):
        at = pl.ds(pl.multiple_of(t * 8, 8), 8)
        acc = [None] * HY
        for i in range(HY + 2 * R):
            value = lines[base + i, at, :]
            for y in range(HY):
                if 0 <= i - y < TAPS:
                    term = tap[i - y] * value
                    acc[y] = term if acc[y] is None else acc[y] + term
        for y in range(HY):
            held[y, at, :] = acc[y]
        return carry

    lax.fori_loop(0, CX // 8, tile, 0)
    high, low = two(held[...].reshape(HY * CX, CZ))
    result = mm(jnp.concatenate([high, high, low], axis=1), band_z[...])
    return [result[y * CX : (y + 1) * CX] for y in range(HY)]


def put_x(xa, xb, padded, count, shared=False):
    odd_x, _ = sides()
    first = 1 - odd_x
    if shared:
        first = jnp.where(lax.axis_index("view") % 2 == 0, first, odd_x)
    padded[:count, pl.ds(pl.multiple_of(first * (CX + R), R), R), :] = xa[...]
    padded[:count, pl.ds(pl.multiple_of((1 - first) * (CX + R), R), R), :] = xb[...]


def put_side(y_halo, padded):
    if len(y_halo) == 2:
        padded[:R, R : R + CX, :] = y_halo[0][...]
        put_x(y_halo[1].at[0], y_halo[1].at[1], padded, R)
    else:
        core = lax.axis_index("view") % 2
        padded[pl.ds(core * (R // 2), R // 2), R : R + CX, :] = y_halo[0][...]
        padded[pl.ds((1 - core) * (R // 2), R // 2), R : R + CX, :] = y_halo[1][...]
        put_x(*y_halo[2:], padded, R, shared=True)


def far_lines(own, x_halos, y_halo, band_x, padded, lines, shared=False):
    _, odd_y = sides()
    padded[:, R : R + CX, :] = own[...]
    put_x(*x_halos, padded, CY, shared)
    smear_x(padded, CY, band_x, lines, R)
    far = (CY + R) * odd_y
    if y_halo:
        put_side(y_halo, padded)
        smear_x(padded, R, band_x, lines, far)
    else:
        lines[pl.ds(far, R)] = jnp.zeros((R, CX, CZ), F32)


def near_lines(y_halo, band_x, padded, lines):
    _, odd_y = sides()
    put_side(y_halo, padded)
    smear_x(padded, R, band_x, lines, (CY + R) * (1 - odd_y))


def blur_far_kernel(own, *refs):
    ins, (out, lines, padded, held) = refs[:-4], refs[-4:]
    halos, (band_x, band_z, taps) = ins[:-3], ins[-3:]
    _, odd_y = sides()
    far_lines(own, halos[:2], halos[2:], band_x, padded, lines, shared=True)
    for y, value in enumerate(smear_yz(lines, HY * odd_y, taps, band_z, held)):
        out[y] = value


def blur_near_kernel(far, before, *refs):
    y_halo, (band_x, band_z, taps, out, padded, held, lines) = refs[:4], refs[4:]
    _, odd_y = sides()
    lines[R : R + CY] = before[R : R + CY]
    near_lines(y_halo, band_x, padded, lines)
    out[pl.ds(HY * odd_y, HY)] = far[...]
    start = HY * (1 - odd_y)
    for y, value in enumerate(smear_yz(lines, start, taps, band_z, held)):
        out[start + y] = value


def put_quarters(values, mine, other, whole):
    core = lax.axis_index("view") % 2
    for y in range(HY):
        whole[pl.ds(y, CX, stride=HY), :] = values[y]
    rows = HX * HY
    other[...] = whole[pl.ds(pl.multiple_of((1 - core) * rows, rows), rows), :]
    mine[...] = whole[pl.ds(pl.multiple_of(core * rows, rows), rows), :]


def far_kernel(own, *refs):
    ins, (mine, other, lines, padded, held, whole) = refs[:-6], refs[-6:]
    halos, (band_x, band_z, taps) = ins[:-3], ins[-3:]
    _, odd_y = sides()
    far_lines(own, halos[-2:], halos[:-2], band_x, padded, lines)
    values = smear_yz(lines, HY * odd_y, taps, band_z, held)
    put_quarters(values, mine, other, whole)


def near_kernel(after, before, *refs):
    halos, (band_x, band_z, taps, mine, other, padded, held, whole, lines) = refs[:2], refs[2:]
    _, odd_y = sides()
    lines[R : R + CY] = before[R : R + CY]
    near_lines(halos, band_x, padded, lines)
    values = smear_yz(lines, HY * (1 - odd_y), taps, band_z, held)
    put_quarters(values, mine, other, whole)


def ratio_kernel(chunks, *refs):
    parts, blurred = refs[:chunks], refs[chunks]
    ratio, *edges = refs[chunks + 1 :]
    rows = chunks * GROUP
    metas = []
    for c in range(0, chunks, 2):
        odd = pltpu.roll(parts[c + 1][YP * GROUP :, :], GROUP, 1)
        metas.append(parts[c][YP * GROUP :, :] + odd)
    meta = jnp.concatenate(metas, axis=1)
    slot, count, weight = meta[0:1].astype(jnp.int32), meta[1:2].astype(jnp.int32), meta[2:3]
    key = (slot & (YP - 1)) * CX + (slot >> 2)
    chooser = (iota((SLOTS, rows), 0) == key).astype(F32).astype(BF16)
    keep = jnp.where(iota((CZ, rows), 0) < count, weight, 0.0).T

    def gathered(values):
        return sum(mm(chooser, part) for part in two(values))

    cover = gathered(keep)
    for j in range(0, YP, 2):
        values = jnp.concatenate(
            [
                jnp.concatenate([p[k * GROUP : (k + 1) * GROUP, :] for p in parts], axis=0)
                for k in (j, j + 1)
            ],
            axis=1,
        )
        data = gathered(values)
        for q in range(CY // YP):
            at = slice(q * CX, (q + 1) * CX)
            for k in range(2):
                y = YP * q + j + k
                base = blurred[y]
                ratio[y] = (data[at, k * CZ : (k + 1) * CZ] + PRIOR_WEIGHT * base) / (
                    (cover[at] + PRIOR_WEIGHT) * base
                )
    put_edges(ratio, edges)


def store_kernel(parts, *refs):
    ins, out, sems = refs[: len(parts)], refs[-2], refs[-1]
    core, (_, odd_y) = lax.axis_index("view") % 2, sides()
    copies = []
    for i, (part, near) in enumerate(parts):
        x = pl.multiple_of(HX * (core if part == 0 else 1 - core), HX)
        y = pl.multiple_of(HY * (1 - odd_y if near else odd_y), HY)
        to = out.at[pl.ds(x, HX), pl.ds(y, HY), :]
        copies.append(pltpu.make_async_copy(ins[i], to, sems.at[i]))
        copies[-1].start()
    for copy in copies:
        copy.wait()


def store(parts, values, before):
    def kernel(*refs):
        store_kernel(parts, *refs)

    values = [value.reshape(HX, HY, CZ) for value in values]
    specs, aliases = [VM] * len(values), {}
    if before is not None:
        values.append(before)
        specs.append(ANY)
        aliases = {len(parts): 0}
    sems = [pltpu.SemaphoreType.DMA((len(parts),))]
    return call(kernel, [(CX, CY, CZ)], sems, specs, [ANY], aliases)(*values)[0]


def swap(x, axis, mask):
    return lax.ppermute(x, axis, [(i, i ^ mask) for i in range(lax.axis_size(axis))])


def pairs(axis):
    count = lax.axis_size(axis)
    first = [(i, i ^ 1) for i in range(count) if i ^ 1 < count]
    second = [(i, ((i + 1) ^ 1) - 1) for i in range(count)]
    second = [(i, k) for i, k in second if 0 <= k < count]
    return [first] + ([second] if second else [])


def halo(edges):
    x_pairs, y_pairs = pairs("bx"), pairs("by")
    x_pairs = x_pairs + [[]] * (2 - len(x_pairs))

    def move(value, axis, moves):
        return lax.ppermute(value, axis, moves) if moves else jnp.zeros_like(value)

    got_y = [move(e, "by", p) for e, p in zip(edges, y_pairs)]
    got_x = [move(e, "bx", p) for e, p in zip(edges[-2:], x_pairs)]
    cut = call(corner_kernel, [(2, R, R, CZ)] * len(y_pairs), in_specs=[VM] * 2)(*got_x)
    got_c = [move(e, "by", p) for e, p in zip(cut, y_pairs)]
    return [value for both in zip(got_y, got_c) for value in both] + got_x


def shared_halo(edge_x, edges_y):
    x_pairs, y_pairs, wide = pairs("bx"), pairs("by"), lax.axis_size("bx")
    x_pairs = x_pairs + [[]] * (2 - len(x_pairs))
    moves = [
        (view * wide + a, view * wide + b)
        for view in range(lax.axis_size("view"))
        for a, b in x_pairs[view % 2]
    ]
    got_x = lax.ppermute(edge_x, ("view", "bx"), moves)
    got_y = []
    for edge, pair in zip(edges_y, y_pairs):
        got_y.append(lax.ppermute(edge, "by", pair))
    cut = call(cut_kernel, [(R, R, CZ)] * len(y_pairs), in_specs=[VM])(got_x)
    out = [got_x, swap(got_x, "view", 1)]
    for y, corner, pair in zip(got_y, cut, y_pairs):
        corner = lax.ppermute(corner, "by", pair)
        out += [y, swap(y, "view", 1), corner, swap(corner, "view", 1)]
    return out


def generic_exchange(bricks, observed, target, slot, count, weight):
    capacity = max(4, 2 * PIECES // bricks)
    member = (target[:, None] == jnp.arange(bricks)[None, :]).astype(jnp.int32)
    slot_rank = jnp.sum((jnp.cumsum(member, axis=0) - 1) * member, axis=1)
    place = target * capacity + slot_rank
    keep = jnp.where(jnp.arange(CZ)[None, :] < count[:, None], weight[:, None], 0.0)
    weighted = (observed.reshape(-1, YP, CZ) * keep[:, None, :]).reshape(-1, PV)
    facts = jnp.stack([slot.astype(F32), count.astype(F32), weight], axis=1)
    rows = jnp.zeros((bricks * capacity, PV), F32).at[place].set(weighted)
    facts = jnp.zeros((bricks * capacity, 3), F32).at[place].set(facts)

    def exchange(x):
        x = x.reshape(bricks, capacity, -1)
        return lax.all_to_all(x, ("bx", "by"), split_axis=0, concat_axis=0, tiled=True)

    chunks = bricks * capacity // GROUP
    rows = exchange(rows).reshape(chunks, GROUP, YP, CZ).transpose(0, 2, 1, 3)
    facts = exchange(facts).reshape(chunks, GROUP, 3).transpose(0, 2, 1)
    facts = jnp.pad(facts, ((0, 0), (0, 5), (0, CZ - GROUP)))
    both = jnp.concatenate([rows.reshape(chunks, YP * GROUP, CZ), facts], axis=1)
    return [both[c] for c in range(chunks)]


def local(
    estimate,
    observed,
    destination,
    slot_index,
    valid_count,
    blend_weight,
    kernel_x,
    kernel_y,
    kernel_z,
):
    count_bx, count_by = lax.axis_size("bx"), lax.axis_size("by")
    bricks = count_bx * count_by
    phases = len(pairs("by"))
    flat = estimate.reshape(CX * CY, CZ)
    edge_shapes = [(R, CX, CZ)] * phases + [(CY, R, CZ)] * 2
    brick, half = (CY, CX, CZ), (HY, CX, CZ)
    quarter, lines = (HX * HY, CZ), (CY + 2 * R, CX, CZ)
    padded, held = pltpu.VMEM((CY, XE, CZ), F32), pltpu.VMEM((HY, CX, CZ), F32)
    whole = pltpu.VMEM((CX * HY, CZ), F32)

    if bricks * GROUP == 2 * PIECES:
        room = [pltpu.VMEM((PIECES, PV), F32)]
        room += [pltpu.VMEM((1, PIECES), jnp.int32)] * 3 + [pltpu.VMEM((1, PIECES), F32)]
        room.append(pltpu.SemaphoreType.DMA((5,)))
        shapes = [(CHUNK, CZ)] * bricks + [(8, CZ)]
        *packed, token = call(pack_kernel, shapes, room, [HB] * 5, limit=PACK_LIMIT)(
            *[
                pltpu.with_memory_space_constraint(x, pltpu.HBM)
                for x in (
                    observed[0],
                    destination.reshape(1, PIECES),
                    slot_index,
                    valid_count,
                    blend_weight,
                )
            ]
        )
        chunks = [packed[0]]
        for s in sorted(range(1, bricks), reverse=True):
            pair = [(d, d ^ s) for d in range(bricks)]
            chunks.append(lax.ppermute(packed[s], ("bx", "by"), pair))
    else:
        token = jnp.zeros((8, CZ), F32)
        chunks = generic_exchange(
            bricks,
            observed[0],
            destination[0, :, 0],
            slot_index[0],
            valid_count[0],
            blend_weight[0],
        )

    shapes = [brick, (CY, R, CZ)] + [(R // 2, CX, CZ)] * phases
    turned, edge_x, *edges_y = call(turn_kernel, shapes, in_specs=[VM, ANY])(flat, token)
    around = shared_halo(edge_x, edges_y)
    shapes = [((CX, 3 * XE), BF16), ((3 * CZ, CZ), BF16), ((ROWS, CZ), F32)] * 2
    shapes = [jax.ShapeDtypeStruct(*shape) for shape in shapes]
    bands = call(band_kernel, shapes, in_specs=[SM] * 3)(kernel_x, kernel_y, kernel_z)
    forward, bands = bands[:3], bands[3:]
    far_halos, near_halos = around[:2] + around[6:], around[2:6]
    blurred, before = call(
        blur_far_kernel, [half, lines], [padded, held], [VM] * (len(far_halos) + 4)
    )(turned, *far_halos, *forward)
    work = [padded, held, pltpu.VMEM(lines, F32)]
    (blurred,) = call(blur_near_kernel, [brick], work, [VM] * 9)(
        blurred, before, *near_halos, *forward
    )

    def ratios(*refs):
        ratio_kernel(len(chunks), *refs)

    ratio, *edges = call(ratios, [brick] + edge_shapes, in_specs=[VM] * (len(chunks) + 1))(
        *chunks, blurred
    )
    around = halo(edges)
    near_halos, far_halos = around[:2], around[2:]
    mine, other, before = call(
        far_kernel,
        [quarter, quarter, lines],
        [padded, held, whole],
        [VM] * (len(far_halos) + 4),
    )(ratio, *far_halos, *bands)
    core, odd_y = lax.axis_index("view") % 2, lax.axis_index("by") % 2

    def paired(mine, other):
        return mine * swap(other, "view", 1)

    def product(mine, start, estimate):
        across = swap(mine, "view", 2)
        own = lax.dynamic_slice(estimate, (core * HX, start * HY, 0), (HX, HY, CZ))
        mine = mine * across * own.reshape(HX * HY, CZ)
        return mine, swap(mine, "view", 1)

    mine = paired(mine, other)
    work = [padded, held, whole, pltpu.VMEM(lines, F32)]
    near = call(near_kernel, [quarter, quarter], work, [ANY] + [VM] * 6)(
        mine, before, *near_halos, *bands
    )
    far_mine, far_other = product(mine, odd_y, estimate)
    updated = store([(0, False), (1, False)], [far_mine, far_other], None)
    estimate, far_mine = lax.optimization_barrier((estimate, far_mine))
    near_mine, near_other = product(paired(*near), 1 - odd_y, estimate)
    updated = store([(0, True)], [near_mine], updated)
    return store([(1, True)], [near_other], updated)


def solution(mesh):
    placed = (
        P("bx", "by", None),
        P("view", ("bx", "by"), None),
        P("view", ("bx", "by"), None),
        P("view", ("bx", "by")),
        P("view", ("bx", "by")),
        P("view", ("bx", "by")),
        P("view", None),
        P("view", None),
        P("view", None),
    )

    return jax.shard_map(
        local, mesh=mesh, in_specs=placed, out_specs=P("bx", "by", None), check_vma=False
    )
```

```python
import jax
import jax.numpy as jnp
from jax import lax
from jax.experimental import pallas as pl
from jax.experimental.pallas import tpu as pltpu
from jax.sharding import PartitionSpec as P


R = 8
RZ = 16
YP = 4
PV = 512
SLOTS = 256
PIECES = 256
CX = 64
CY = 16
CZ = 128
PRIOR_WEIGHT = 0.5
F32 = jnp.float32
BF16 = jnp.bfloat16
VM = pl.BlockSpec(memory_space=pltpu.VMEM)
SM = pl.BlockSpec(memory_space=pltpu.SMEM)
ANY = pl.BlockSpec(memory_space=pl.ANY)
HB = pl.BlockSpec(memory_space=pltpu.HBM)
HX = CX // 2
HY = CY // 2
XE = CX + 2 * R
TAPS = 2 * R + 1
ROWS = 24
PACK_LIMIT = 32 << 20
GROUP = 64
CHUNK = YP * GROUP + 8


def call(
    kernel,
    outs,
    scratch=(),
    in_specs=None,
    out_specs=None,
    aliases=None,
    limit=32 << 20,
    flops=1 << 22,
    moved=1 << 20,
):
    shapes = [o if hasattr(o, "dtype") else jax.ShapeDtypeStruct(o, F32) for o in outs]
    return pl.pallas_call(
        kernel,
        out_shape=shapes,
        in_specs=in_specs,
        out_specs=out_specs or [VM] * len(outs),
        scratch_shapes=list(scratch),
        input_output_aliases=aliases or {},
        compiler_params=pltpu.CompilerParams(vmem_limit_bytes=limit),
        cost_estimate=pl.CostEstimate(flops=flops, bytes_accessed=moved, transcendentals=0),
    )


def three(x):
    high = x.astype(BF16)
    rest = x - high.astype(F32)
    mid = rest.astype(BF16)
    return high, mid, (rest - mid.astype(F32)).astype(BF16)


def two(x):
    high = x.astype(BF16)
    return high, (x - high.astype(F32)).astype(BF16)


def iota(shape, dim):
    return lax.broadcasted_iota(jnp.int32, shape, dim)


def mm(a, b):
    return jnp.dot(a, b, preferred_element_type=F32)


def pack_kernel(*refs):
    sources, outs, token, held, sems = refs[:5], refs[5:-7], refs[-7], refs[-6:-1], refs[-1]
    bricks = len(outs)
    token[...] = jnp.zeros((8, CZ), F32)
    copies = [
        pltpu.make_async_copy(source, to, sems.at[i])
        for i, (source, to) in enumerate(zip(sources, held))
    ]
    for copy in copies:
        copy.start()
    observed, target, slot, count, weight = held
    for copy in copies[1:]:
        copy.wait()
    me = lax.axis_index("bx") * lax.axis_size("by") + lax.axis_index("by")
    goal = target[...] ^ me
    member = (iota((bricks, PIECES), 0) == goal).astype(F32)
    upto = (iota((PIECES, PIECES), 0) <= iota((PIECES, PIECES), 1)).astype(F32)
    ranks = mm(member.astype(BF16), upto.astype(BF16))
    rank = jnp.sum(member * ranks, axis=0, keepdims=True).astype(jnp.int32) - 1
    place = goal * GROUP + rank
    rows = bricks * GROUP
    pick = (iota((rows, PIECES), 0) == place).astype(F32).astype(BF16)
    keep = jnp.where(iota((CZ, PIECES), 0) < count[...], weight[...], 0.0).T
    copies[0].wait()
    weighted = observed[...] * jnp.concatenate([keep] * YP, axis=1)
    packed = sum(mm(pick, part) for part in three(weighted))
    parts = [p.astype(F32) for p in three(weight[...])]
    table = jnp.concatenate(
        [slot[...].astype(F32), count[...].astype(F32)] + parts + [jnp.zeros((3, PIECES), F32)],
        axis=0,
    )
    meta = lax.dot_general(
        table.astype(BF16), pick, (((1,), (1,)), ((), ())), preferred_element_type=F32
    )
    wide = jnp.concatenate(
        [meta[0:2], meta[2:3] + meta[3:4] + meta[4:5], jnp.zeros((5, rows), F32)], axis=0
    )
    lane = iota((8, CZ), 1)
    for s in range(bricks):
        for j in range(YP):
            outs[s][j * GROUP : (j + 1) * GROUP, :] = packed[
                s * GROUP : (s + 1) * GROUP, j * CZ : (j + 1) * CZ
            ]
        pair = wide[:, (s // 2) * CZ : (s // 2 + 1) * CZ]
        if s % 2:
            pair = pltpu.roll(pair, GROUP, 1)
        outs[s][YP * GROUP :, :] = jnp.where(lane < GROUP, pair, 0.0)


def sides():
    odd_x = lax.axis_index("bx") % 2
    odd_y = lax.axis_index("by") % 2
    return odd_x, odd_y


def put_edges(volume, outs):
    odd_x, odd_y = sides()
    for phase, out in enumerate(outs[:-2]):
        out[...] = volume[pl.ds((odd_y if phase else 1 - odd_y) * (CY - R), R)]
    for phase, out in enumerate(outs[-2:]):
        at = (odd_x if phase else 1 - odd_x) * (CX - R)
        out[...] = volume[:, pl.ds(pl.multiple_of(at, R), R), :]


def corner_kernel(xa, xb, *outs):
    _, odd_y = sides()
    for phase, out in enumerate(outs):
        rows = pl.ds((odd_y if phase else 1 - odd_y) * (CY - R), R)
        out[0] = xa[rows]
        out[1] = xb[rows]


def turn_kernel(estimate, after, turned, edge_x, *edges_y):
    for y in range(CY):
        turned[y] = estimate[pl.ds(y, CX, stride=CY), :]
    odd_x, odd_y = sides()
    core = lax.axis_index("view") % 2
    at = jnp.where(core == 0, 1 - odd_x, odd_x) * (CX - R)
    edge_x[...] = turned[:, pl.ds(pl.multiple_of(at, R), R), :]
    for phase, out in enumerate(edges_y):
        at = (odd_y if phase else 1 - odd_y) * (CY - R) + core * (R // 2)
        out[...] = turned[pl.ds(at, R // 2)]


def cut_kernel(got, *outs):
    _, odd_y = sides()
    for phase, out in enumerate(outs):
        out[...] = got[pl.ds((odd_y if phase else 1 - odd_y) * (CY - R), R)]


def total(kernel, taps):
    acc = kernel[0, 0]
    for i in range(1, taps):
        acc = acc + kernel[0, i]
    return acc


def band_kernel(kx, ky, kz, *outs):
    ztaps = 2 * RZ + 1
    for reverse in range(2):
        band_x, band_z, taps = outs[3 * reverse : 3 * reverse + 3]
        col, row = iota((CX, 3 * XE), 1), iota((CX, 3 * XE), 0)
        block = jnp.where(col >= 2 * XE, 2, jnp.where(col >= XE, 1, 0))
        gap = col - block * XE - row
        band = jnp.zeros((CX, 3 * XE), F32)
        for i in range(TAPS):
            band = jnp.where(gap == i, kx[0, TAPS - 1 - i if reverse else i], band)
        high, low = two(band / total(kx, TAPS))
        band_x[...] = jnp.where(block == 1, low.astype(F32), high.astype(F32)).astype(BF16)
        gap = iota((CZ, CZ), 0) - iota((CZ, CZ), 1) + RZ
        band = jnp.zeros((CZ, CZ), F32)
        for i in range(ztaps):
            band = jnp.where(gap == i, kz[0, ztaps - 1 - i if reverse else i], band)
        high, low = two(band / total(kz, ztaps))
        band_z[...] = jnp.concatenate([high, low, high], axis=0)
        row = iota((ROWS, CZ), 0)
        table = jnp.zeros((ROWS, CZ), F32)
        for i in range(TAPS):
            table = jnp.where(row == i, ky[0, TAPS - 1 - i if reverse else i], table)
        taps[...] = table / total(ky, TAPS)


def smear_x(padded, count, band_x, lines, base):
    for y in range(0, count, 2):
        stack = []
        for k in range(2):
            high, low = two(padded[y + k])
            stack.append(jnp.concatenate([high, high, low], axis=0))
        both = mm(band_x[...], jnp.concatenate(stack, axis=1))
        lines[base + y] = both[:, :CZ]
        lines[base + y + 1] = both[:, CZ:]


def smear_yz(lines, base, taps, band_z, held, first=0, width=CX):
    tap = [taps[i : i + 1, :] for i in range(TAPS)]

    def tile(t, carry):
        at = pl.ds(pl.multiple_of(first + t * 8, 8), 8)
        acc = [None] * HY
        for i in range(HY + 2 * R):
            value = lines[base + i, at, :]
            for y in range(HY):
                if 0 <= i - y < TAPS:
                    term = tap[i - y] * value
                    acc[y] = term if acc[y] is None else acc[y] + term
        for y in range(HY):
            held[y, pl.ds(pl.multiple_of(t * 8, 8), 8), :] = acc[y]
        return carry

    lax.fori_loop(0, width // 8, tile, 0)
    high, low = two(held[:, :width, :].reshape(HY * width, CZ))
    result = mm(jnp.concatenate([high, high, low], axis=1), band_z[...])
    return [result[y * width : (y + 1) * width] for y in range(HY)]


def put_x(xa, xb, padded, count, shared=False):
    odd_x, _ = sides()
    first = 1 - odd_x
    if shared:
        first = jnp.where(lax.axis_index("view") % 2 == 0, first, odd_x)
    padded[:count, pl.ds(pl.multiple_of(first * (CX + R), R), R), :] = xa[...]
    padded[:count, pl.ds(pl.multiple_of((1 - first) * (CX + R), R), R), :] = xb[...]


def put_side(y_halo, padded):
    if len(y_halo) == 2:
        padded[:R, R : R + CX, :] = y_halo[0][...]
        put_x(y_halo[1].at[0], y_halo[1].at[1], padded, R)
    else:
        core = lax.axis_index("view") % 2
        padded[pl.ds(core * (R // 2), R // 2), R : R + CX, :] = y_halo[0][...]
        padded[pl.ds((1 - core) * (R // 2), R // 2), R : R + CX, :] = y_halo[1][...]
        put_x(*y_halo[2:], padded, R, shared=True)


def far_lines(own, x_halos, y_halo, band_x, padded, lines, shared=False):
    _, odd_y = sides()
    padded[:, R : R + CX, :] = own[...]
    put_x(*x_halos, padded, CY, shared)
    smear_x(padded, CY, band_x, lines, R)
    far = (CY + R) * odd_y
    if y_halo:
        put_side(y_halo, padded)
        smear_x(padded, R, band_x, lines, far)
    else:
        lines[pl.ds(far, R)] = jnp.zeros((R, CX, CZ), F32)


def near_lines(y_halo, band_x, padded, lines):
    _, odd_y = sides()
    put_side(y_halo, padded)
    smear_x(padded, R, band_x, lines, (CY + R) * (1 - odd_y))


def blur_far_kernel(own, *refs):
    ins, (out, lines, padded, held) = refs[:-4], refs[-4:]
    halos, (band_x, band_z, taps) = ins[:-3], ins[-3:]
    _, odd_y = sides()
    far_lines(own, halos[:2], halos[2:], band_x, padded, lines, shared=True)
    for y, value in enumerate(smear_yz(lines, HY * odd_y, taps, band_z, held)):
        out[y] = value


def blur_near_kernel(far, before, *refs):
    y_halo, (band_x, band_z, taps, out, padded, held, lines) = refs[:4], refs[4:]
    _, odd_y = sides()
    lines[R : R + CY] = before[R : R + CY]
    near_lines(y_halo, band_x, padded, lines)
    out[pl.ds(HY * odd_y, HY)] = far[...]
    start = HY * (1 - odd_y)
    for y, value in enumerate(smear_yz(lines, start, taps, band_z, held)):
        out[start + y] = value


def put_quarter(part, near, lines, taps, band_z, out, held):
    core, (_, odd_y) = lax.axis_index("view") % 2, sides()
    base = HY * (1 - odd_y if near else odd_y)
    start = HX * (1 - core if part else core)
    values = smear_yz(lines, base, taps, band_z, held, start, HX)
    for y in range(HY):
        out[pl.ds(y, HX, stride=HY), :] = values[y]


def far_kernel(own, *refs):
    ins, (other, lines, padded, held) = refs[:-4], refs[-4:]
    halos, (band_x, band_z, taps) = ins[:-3], ins[-3:]
    far_lines(own, halos[-2:], halos[:-2], band_x, padded, lines)
    put_quarter(1, False, lines, taps, band_z, other, held)


def near_kernel(after, before, *refs):
    halos, (band_x, band_z, taps, other, lines, padded, held) = refs[:2], refs[2:]
    lines[R : R + CY] = before[R : R + CY]
    near_lines(halos, band_x, padded, lines)
    put_quarter(1, True, lines, taps, band_z, other, held)


def rest(near, lines, band_z, taps, held):
    def kernel(lines, band_z, taps, out, held):
        put_quarter(0, near, lines, taps, band_z, out, held)

    return call(kernel, [(HX * HY, CZ)], [held], [VM] * 3)(lines, band_z, taps)[0]


def ratio_kernel(chunks, *refs):
    parts, blurred = refs[:chunks], refs[chunks]
    ratio, *edges = refs[chunks + 1 :]
    rows = chunks * GROUP
    metas = []
    for c in range(0, chunks, 2):
        odd = pltpu.roll(parts[c + 1][YP * GROUP :, :], GROUP, 1)
        metas.append(parts[c][YP * GROUP :, :] + odd)
    meta = jnp.concatenate(metas, axis=1)
    slot, count, weight = meta[0:1].astype(jnp.int32), meta[1:2].astype(jnp.int32), meta[2:3]
    key = (slot & (YP - 1)) * CX + (slot >> 2)
    chooser = (iota((SLOTS, rows), 0) == key).astype(F32).astype(BF16)
    keep = jnp.where(iota((CZ, rows), 0) < count, weight, 0.0).T

    def gathered(values):
        return sum(mm(chooser, part) for part in two(values))

    both = mm(chooser, jnp.concatenate(two(keep), axis=1))
    cover = both[:, :CZ] + both[:, CZ:]
    for j in range(0, YP, 2):
        values = jnp.concatenate(
            [
                jnp.concatenate([p[k * GROUP : (k + 1) * GROUP, :] for p in parts], axis=0)
                for k in (j, j + 1)
            ],
            axis=1,
        )
        data = gathered(values)
        for q in range(CY // YP):
            at = slice(q * CX, (q + 1) * CX)
            for k in range(2):
                y = YP * q + j + k
                base = blurred[y]
                ratio[y] = (data[at, k * CZ : (k + 1) * CZ] + PRIOR_WEIGHT * base) / (
                    (cover[at] + PRIOR_WEIGHT) * base
                )
    put_edges(ratio, edges)


def store_kernel(parts, *refs):
    ins, out, sems = refs[: len(parts)], refs[-2], refs[-1]
    core, (_, odd_y) = lax.axis_index("view") % 2, sides()
    copies = []
    for i, (part, near) in enumerate(parts):
        x = pl.multiple_of(HX * (core if part == 0 else 1 - core), HX)
        y = pl.multiple_of(HY * (1 - odd_y if near else odd_y), HY)
        to = out.at[pl.ds(x, HX), pl.ds(y, HY), :]
        copies.append(pltpu.make_async_copy(ins[i], to, sems.at[i]))
        copies[-1].start()
    for copy in copies:
        copy.wait()


def store(parts, values, before):
    def kernel(*refs):
        store_kernel(parts, *refs)

    values = [value.reshape(HX, HY, CZ) for value in values]
    specs, aliases = [VM] * len(values), {}
    if before is not None:
        values.append(before)
        specs.append(ANY)
        aliases = {len(parts): 0}
    sems = [pltpu.SemaphoreType.DMA((len(parts),))]
    return call(kernel, [(CX, CY, CZ)], sems, specs, [ANY], aliases)(*values)[0]


def swap(x, axis, mask):
    return lax.ppermute(x, axis, [(i, i ^ mask) for i in range(lax.axis_size(axis))])


def pairs(axis):
    count = lax.axis_size(axis)
    first = [(i, i ^ 1) for i in range(count) if i ^ 1 < count]
    second = [(i, ((i + 1) ^ 1) - 1) for i in range(count)]
    second = [(i, k) for i, k in second if 0 <= k < count]
    return [first] + ([second] if second else [])


def halo(edges):
    x_pairs, y_pairs = pairs("bx"), pairs("by")
    x_pairs = x_pairs + [[]] * (2 - len(x_pairs))

    def move(value, axis, moves):
        return lax.ppermute(value, axis, moves) if moves else jnp.zeros_like(value)

    got_y = [move(e, "by", p) for e, p in zip(edges, y_pairs)]
    got_x = [move(e, "bx", p) for e, p in zip(edges[-2:], x_pairs)]
    cut = call(corner_kernel, [(2, R, R, CZ)] * len(y_pairs), in_specs=[VM] * 2)(*got_x)
    got_c = [move(e, "by", p) for e, p in zip(cut, y_pairs)]
    return [value for both in zip(got_y, got_c) for value in both] + got_x


def shared_halo(edge_x, edges_y):
    x_pairs, y_pairs, wide = pairs("bx"), pairs("by"), lax.axis_size("bx")
    x_pairs = x_pairs + [[]] * (2 - len(x_pairs))
    moves = [
        (view * wide + a, view * wide + b)
        for view in range(lax.axis_size("view"))
        for a, b in x_pairs[view % 2]
    ]
    got_x = lax.ppermute(edge_x, ("view", "bx"), moves)
    got_y = []
    for edge, pair in zip(edges_y, y_pairs):
        got_y.append(lax.ppermute(edge, "by", pair))
    cut = call(cut_kernel, [(R, R, CZ)] * len(y_pairs), in_specs=[VM])(got_x)
    out = [got_x, swap(got_x, "view", 1)]
    for y, corner, pair in zip(got_y, cut, y_pairs):
        corner = lax.ppermute(corner, "by", pair)
        out += [y, swap(y, "view", 1), corner, swap(corner, "view", 1)]
    return out


def generic_exchange(bricks, observed, target, slot, count, weight):
    capacity = max(4, 2 * PIECES // bricks)
    member = (target[:, None] == jnp.arange(bricks)[None, :]).astype(jnp.int32)
    slot_rank = jnp.sum((jnp.cumsum(member, axis=0) - 1) * member, axis=1)
    place = target * capacity + slot_rank
    keep = jnp.where(jnp.arange(CZ)[None, :] < count[:, None], weight[:, None], 0.0)
    weighted = (observed.reshape(-1, YP, CZ) * keep[:, None, :]).reshape(-1, PV)
    facts = jnp.stack([slot.astype(F32), count.astype(F32), weight], axis=1)
    rows = jnp.zeros((bricks * capacity, PV), F32).at[place].set(weighted)
    facts = jnp.zeros((bricks * capacity, 3), F32).at[place].set(facts)

    def exchange(x):
        x = x.reshape(bricks, capacity, -1)
        return lax.all_to_all(x, ("bx", "by"), split_axis=0, concat_axis=0, tiled=True)

    chunks = bricks * capacity // GROUP
    rows = exchange(rows).reshape(chunks, GROUP, YP, CZ).transpose(0, 2, 1, 3)
    facts = exchange(facts).reshape(chunks, GROUP, 3).transpose(0, 2, 1)
    facts = jnp.pad(facts, ((0, 0), (0, 5), (0, CZ - GROUP)))
    both = jnp.concatenate([rows.reshape(chunks, YP * GROUP, CZ), facts], axis=1)
    return [both[c] for c in range(chunks)]


def local(
    estimate,
    observed,
    destination,
    slot_index,
    valid_count,
    blend_weight,
    kernel_x,
    kernel_y,
    kernel_z,
):
    count_bx, count_by = lax.axis_size("bx"), lax.axis_size("by")
    bricks = count_bx * count_by
    phases = len(pairs("by"))
    flat = estimate.reshape(CX * CY, CZ)
    edge_shapes = [(R, CX, CZ)] * phases + [(CY, R, CZ)] * 2
    brick, half = (CY, CX, CZ), (HY, CX, CZ)
    quarter, lines = (HX * HY, CZ), (CY + 2 * R, CX, CZ)
    padded, held = pltpu.VMEM((CY, XE, CZ), F32), pltpu.VMEM((HY, CX, CZ), F32)

    if bricks * GROUP == 2 * PIECES:
        room = [pltpu.VMEM((PIECES, PV), F32)]
        room += [pltpu.VMEM((1, PIECES), jnp.int32)] * 3 + [pltpu.VMEM((1, PIECES), F32)]
        room.append(pltpu.SemaphoreType.DMA((5,)))
        shapes = [(CHUNK, CZ)] * bricks + [(8, CZ)]
        *packed, token = call(pack_kernel, shapes, room, [HB] * 5, limit=PACK_LIMIT)(
            *[
                pltpu.with_memory_space_constraint(x, pltpu.HBM)
                for x in (
                    observed[0],
                    destination.reshape(1, PIECES),
                    slot_index,
                    valid_count,
                    blend_weight,
                )
            ]
        )
        chunks = [packed[0]]
        for s in sorted(range(1, bricks), reverse=True):
            pair = [(d, d ^ s) for d in range(bricks)]
            chunks.append(lax.ppermute(packed[s], ("bx", "by"), pair))
    else:
        token = jnp.zeros((8, CZ), F32)
        chunks = generic_exchange(
            bricks,
            observed[0],
            destination[0, :, 0],
            slot_index[0],
            valid_count[0],
            blend_weight[0],
        )

    shapes = [brick, (CY, R, CZ)] + [(R // 2, CX, CZ)] * phases
    turned, edge_x, *edges_y = call(turn_kernel, shapes, in_specs=[VM, ANY])(flat, token)
    around = shared_halo(edge_x, edges_y)
    shapes = [((CX, 3 * XE), BF16), ((3 * CZ, CZ), BF16), ((ROWS, CZ), F32)] * 2
    shapes = [jax.ShapeDtypeStruct(*shape) for shape in shapes]
    bands = call(band_kernel, shapes, in_specs=[SM] * 3)(kernel_x, kernel_y, kernel_z)
    forward, bands = bands[:3], bands[3:]
    far_halos, near_halos = around[:2] + around[6:], around[2:6]
    blurred, before = call(
        blur_far_kernel, [half, lines], [padded, held], [VM] * (len(far_halos) + 4)
    )(turned, *far_halos, *forward)
    work = [padded, held, pltpu.VMEM(lines, F32)]
    (blurred,) = call(blur_near_kernel, [brick], work, [VM] * 9)(
        blurred, before, *near_halos, *forward
    )

    def ratios(*refs):
        ratio_kernel(len(chunks), *refs)

    ratio, *edges = call(ratios, [brick] + edge_shapes, in_specs=[VM] * (len(chunks) + 1))(
        *chunks, blurred
    )
    around = halo(edges)
    near_halos, far_halos = around[:2], around[2:]
    other, before = call(
        far_kernel,
        [quarter, lines],
        [padded, held],
        [VM] * (len(far_halos) + 4),
    )(ratio, *far_halos, *bands)
    core, odd_y = lax.axis_index("view") % 2, lax.axis_index("by") % 2

    def paired(mine, other):
        return mine * swap(other, "view", 1)

    def product(mine, start, estimate):
        across = swap(mine, "view", 2)
        own = lax.dynamic_slice(estimate, (core * HX, start * HY, 0), (HX, HY, CZ))
        mine = mine * across * own.reshape(HX * HY, CZ)
        return mine, swap(mine, "view", 1)

    mine = paired(rest(False, before, *bands[1:], held), other)
    other, after = call(near_kernel, [quarter, lines], [padded, held], [ANY] + [VM] * 6)(
        mine, before, *near_halos, *bands
    )
    far_mine, far_other = product(mine, odd_y, estimate)
    updated = store([(0, False), (1, False)], [far_mine, far_other], None)
    estimate, far_mine = lax.optimization_barrier((estimate, far_mine))
    mine = paired(rest(True, after, *bands[1:], held), other)
    near_mine, near_other = product(mine, 1 - odd_y, estimate)
    updated = store([(0, True)], [near_mine], updated)
    return store([(1, True)], [near_other], updated)


def solution(mesh):
    placed = (
        P("bx", "by", None),
        P("view", ("bx", "by"), None),
        P("view", ("bx", "by"), None),
        P("view", ("bx", "by")),
        P("view", ("bx", "by")),
        P("view", ("bx", "by")),
        P("view", None),
        P("view", None),
        P("view", None),
    )

    return jax.shard_map(
        local, mesh=mesh, in_specs=placed, out_specs=P("bx", "by", None), check_vma=False
    )
```
